256 devices in a mesh: head: 16 (over y_lo, z), query: 16 (over y_hi, x, core).
Axes of the slice: x: 4, y: 4 (y_hi: 2, y_lo: 2; y = y_hi * 2 + y_lo), z: 8, core: 2. Of those that a mesh axis runs over, the one named last changes fastest.
Arguments:
- queries: bfloat16 [16384, 32, 128], P(('query', 'head')), may hold values from -100 to 100
- keys: bfloat16 [16384, 4, 128], P(('query', 'head')), may hold values from -4 to 4
- values: bfloat16 [16384, 4, 128], P(('query', 'head')), may hold values from -6 to 6
- attention_out: bfloat16 [16384, 32, 128], P(('query', 'head')), may hold values from -3 to 3
- out_grad: bfloat16 [16384, 32, 128], P(('query', 'head')), may hold values from -6 to 6
- span_order: int32 [16, 2], replicated, may hold values from 0 to 31, as said below
- doc_lengths: int32 [64], replicated, may hold values from 1 to 512, 16384 in all
Outputs:
- query_grad: bfloat16 [16384, 32, 128], P(('query', 'head'))
- key_grad: bfloat16 [16384, 4, 128], P(('query', 'head'))
- value_grad: bfloat16 [16384, 4, 128], P(('query', 'head'))
The draws below stay inside these ranges and needn't reach their ends.
Inputs may be any that keep to these rules, and one draw needn't show every extreme that they name: `span_order`: every number from 0 to 31 appears exactly once; the two numbers of a row sum to 31, in either order. `doc_lengths`: the lengths sum to 16384.
All inputs are finite; a program needn't handle non-finite values.
Results may differ from the reference program's by a relative error of at most 0.0058.
Values may be sent and summed in bfloat16 or wider, within the bound.
No kernel may reach another device: no remote copies, remote signals or barrier semaphores. Data moves between devices by JAX's collectives and lax.ppermute only.
A program may use at most 128 MiB of HBM per device.

```python
import math
import jax
import jax.numpy as jnp
import numpy as np
from jax import lax

QUERY_HEADS = 32
KEY_VALUE_HEADS = 4
HEAD_WIDTH = 128
GROUP = 8
QROWS = 1024
TOKEN_COUNT = 16384
SPAN = 512
DOC_MOST = 512
DOCS = 64
N_HEAD = 16


def drawn_pair(key):
    base = jax.random.fold_in(key, 7)
    random_key_seed, query_seed = jax.random.split(base, 2)
    sampled_keys = jnp.clip(jax.random.normal(random_key_seed, (TOKEN_COUNT, KEY_VALUE_HEADS, HEAD_WIDTH), jnp.float32), -4.0, 4.0)
    queries_draw = jnp.clip(jax.random.normal(query_seed, (TOKEN_COUNT, QUERY_HEADS, HEAD_WIDTH), jnp.float32), -4.0, 4.0)
    return (queries_draw, sampled_keys)


def draw_queries(key, part):
    return drawn_pair(key)[0].astype(jnp.bfloat16)


def draw_keys(key, part):
    return drawn_pair(key)[1].astype(jnp.bfloat16)


def draw_span_order(key, part):
    pair_count = TOKEN_COUNT // QROWS
    order_seed, swap_seed = jax.random.split(jax.random.fold_in(key, 11))
    early_span = jax.random.permutation(order_seed, jnp.arange(pair_count, dtype=jnp.int32))
    late_span = 2 * pair_count - 1 - early_span
    swapped = jax.random.randint(swap_seed, (pair_count,), 0, 2)
    leading = jnp.where(swapped == 1, late_span, early_span)
    trailing = jnp.where(swapped == 1, early_span, late_span)
    return jnp.stack([leading, trailing], axis=1).astype(jnp.int32)


def block_scale(stream_key, extent, cuts, smallest, largest):
    level, own = 1.0, jax.random.fold_in(stream_key, 6)
    for axis_at, shards_of in cuts:
        draws = jnp.exp(jax.random.uniform(jax.random.fold_in(own, axis_at), (shards_of,), jnp.float32, smallest / len(cuts), largest / len(cuts)))
        level = level * jnp.repeat(draws, extent[axis_at] // shards_of).reshape([-1 if axis == axis_at else 1 for axis in range(len(extent))])
    return level


def length_profile(number_of, total, most, lean):
    portions = [(1 << 20) // math.isqrt(rank ** lean) + 1 for rank in range(2, number_of + 1)]
    spare, counts = total - most - (number_of - 1), [1] * (number_of - 1)
    while spare > 0:
        free = [i for i in range(number_of - 1) if counts[i] < most]
        mass, remaining = sum([portions[i] for i in free]), spare
        for i in free:
            addition = min(most - counts[i], max(1, remaining * portions[i] // mass), spare)
            counts[i] = counts[i] + addition
            spare = spare - addition
    return np.array([most] + counts)


def ragged(rng, number_of, total, bound, slope):
    if number_of == 2:
        one = jax.random.randint(rng, (), max(1, total - bound), min(bound, total - 1) + 1)
        return jnp.stack([one, total - one])
    tallies = jnp.asarray(length_profile(number_of, total, bound, slope), jnp.int32)
    pairs = (number_of - 1) // 2
    source_of, receiver = tallies[1:1 + 2 * pairs:2], tallies[2:2 + 2 * pairs:2]
    margin = jnp.minimum(source_of - 1, bound - receiver)
    passed = jax.random.randint(jax.random.fold_in(rng, 1), (pairs,), 0, 1 << 20) % (margin + 1)
    tallies = tallies.at[1:1 + 2 * pairs:2].set(source_of - passed).at[2:2 + 2 * pairs:2].set(receiver + passed)
    return tallies[jax.random.permutation(jax.random.fold_in(rng, 2), number_of)]


def scatter_about(stream_key, extent, scale, reach, cuts=(), kind=jnp.bfloat16):
    drawn = jax.random.normal(stream_key, extent, jnp.float32) * scale
    if len(cuts) > 0:
        drawn = block_scale(stream_key, extent, cuts, -0.22, 0.18) * drawn
    return jnp.clip(drawn, min=-reach, max=reach).astype(kind)


def setup_inputs(seed: int = 0) -> dict:
    arg_keys = jax.random.split(jax.random.key(seed), 8)
    queries = draw_queries(jax.random.fold_in(arg_keys[7], 71), 0)
    keys = draw_keys(jax.random.fold_in(arg_keys[7], 71), 0)
    values = scatter_about(arg_keys[2], (TOKEN_COUNT, KEY_VALUE_HEADS, HEAD_WIDTH), 1.0, 6.0, ((0, 256),))
    attention_out = scatter_about(arg_keys[3], (TOKEN_COUNT, QUERY_HEADS, HEAD_WIDTH), 0.5, 3.0, ((0, 256),))
    out_grad = scatter_about(arg_keys[4], (TOKEN_COUNT, QUERY_HEADS, HEAD_WIDTH), 1.0, 6.0, ((0, 256),))
    span_order = draw_span_order(jax.random.fold_in(arg_keys[7], 71), 0)
    doc_lengths = ragged(arg_keys[6], DOCS, TOKEN_COUNT, DOC_MOST, 2).astype(jnp.int32)
    return {"queries": queries, "keys": keys, "values": values, "attention_out": attention_out, "out_grad": out_grad, "span_order": span_order, "doc_lengths": doc_lengths}


masked = -1e30


def positions(span_order, doc_lengths, rows_each):
    span_rows = rows_each // 2
    within = jnp.arange(span_rows, dtype=jnp.int32)
    pos_all = (span_order[:, :, None] * span_rows + within[None, None, :]).reshape(-1).astype(jnp.int32)
    doc_ends = jnp.cumsum(doc_lengths)[:-1]
    doc_all = jnp.sum((pos_all[:, None] >= doc_ends[None, :]).astype(jnp.int32), axis=1).astype(jnp.int32)
    return pos_all, doc_all


def reference(queries, keys, values, attention_out, out_grad, span_order, doc_lengths):
    pos_all, doc_all = positions(span_order, doc_lengths, QROWS)
    row_of = jnp.zeros((TOKEN_COUNT,), jnp.int32).at[pos_all].set(jnp.arange(TOKEN_COUNT, dtype=jnp.int32))
    doc_sorted = doc_all[row_of]
    window = min(TOKEN_COUNT, SPAN + DOC_MOST)
    span_count = TOKEN_COUNT // SPAN
    factor = HEAD_WIDTH ** -0.5
    head_copies = max(N_HEAD // KEY_VALUE_HEADS, 1)

    def per_head(head):
        kv_index = head // GROUP
        query_pos = queries[:, head, :][row_of]
        key_pos = keys[:, kv_index, :][row_of]
        value_pos = values[:, kv_index, :][row_of]
        grad_pos = out_grad[:, head, :][row_of]
        out_pos = attention_out[:, head, :][row_of]
        delta_pos = jnp.sum(out_pos.astype(jnp.float32) * grad_pos.astype(jnp.float32), axis=-1)

        def step(carry, span):
            key_acc, value_acc = carry
            first = (span * SPAN).astype(jnp.int32)
            start = jnp.clip(first + SPAN - window, 0, TOKEN_COUNT - window).astype(jnp.int32)
            query_mat = lax.dynamic_slice_in_dim(query_pos, first, SPAN)
            grad_mat = lax.dynamic_slice_in_dim(grad_pos, first, SPAN)
            delta = lax.dynamic_slice_in_dim(delta_pos, first, SPAN)
            query_doc = lax.dynamic_slice_in_dim(doc_sorted, first, SPAN)
            key_mat = lax.dynamic_slice_in_dim(key_pos, start, window)
            value_mat = lax.dynamic_slice_in_dim(value_pos, start, window)
            key_doc = lax.dynamic_slice_in_dim(doc_sorted, start, window)
            query_place = first + jnp.arange(SPAN, dtype=jnp.int32)
            key_place = start + jnp.arange(window, dtype=jnp.int32)
            allowed = (key_place[None, :] <= query_place[:, None]) & (key_doc[None, :] == query_doc[:, None])
            scores = jnp.where(allowed, jnp.dot(query_mat, key_mat.T, preferred_element_type=jnp.float32) * factor, masked)
            row_max = jnp.max(scores, axis=-1)
            row_sum = jnp.sum(jnp.where(allowed, jnp.exp(scores - row_max[:, None]), 0.0), axis=-1)
            log_sum = row_max + jnp.log(row_sum)
            probability = jnp.where(allowed, jnp.exp(scores - log_sum[:, None]), 0.0)
            grad_prob = jnp.dot(grad_mat, value_mat.T, preferred_element_type=jnp.float32)
            grad_score = (probability * (grad_prob - delta[:, None])).astype(jnp.bfloat16)
            query_part = jnp.dot(grad_score, key_mat, preferred_element_type=jnp.float32) * factor
            key_part = jnp.dot(grad_score.T, query_mat, preferred_element_type=jnp.float32) * factor
            value_part = jnp.dot(probability.astype(jnp.bfloat16).T, grad_mat, preferred_element_type=jnp.float32)
            key_acc = lax.dynamic_update_slice_in_dim(key_acc, lax.dynamic_slice_in_dim(key_acc, start, window) + key_part, start, 0)
            value_acc = lax.dynamic_update_slice_in_dim(value_acc, lax.dynamic_slice_in_dim(value_acc, start, window) + value_part, start, 0)
            return (key_acc, value_acc), query_part

        zero = jnp.zeros((TOKEN_COUNT, HEAD_WIDTH), jnp.float32)
        (key_acc, value_acc), query_parts = lax.scan(step, (zero, zero), jnp.arange(span_count, dtype=jnp.int32))
        query_sorted = query_parts.reshape(TOKEN_COUNT, HEAD_WIDTH)
        return query_sorted[pos_all], key_acc[pos_all], value_acc[pos_all]

    query_all, key_all, value_all = lax.map(per_head, jnp.arange(QUERY_HEADS, dtype=jnp.int32))

    def collect(gradient_list):
        value_partial = gradient_list.reshape(KEY_VALUE_HEADS, head_copies, QUERY_HEADS // (KEY_VALUE_HEADS * head_copies), TOKEN_COUNT, HEAD_WIDTH).sum(axis=2)
        value_partial = lax.optimization_barrier(value_partial.astype(jnp.bfloat16)).astype(jnp.float32)
        return jnp.transpose(value_partial.sum(axis=1), (1, 0, 2)).astype(jnp.bfloat16)

    query_grad = jnp.transpose(query_all, (1, 0, 2)).astype(jnp.bfloat16)
    return query_grad, collect(key_all), collect(value_all)
```

```python
import jax
import jax.numpy as jnp
from jax import lax
from jax.experimental import pallas as pl
from jax.experimental.pallas import tpu as pltpu
from jax.sharding import Mesh, PartitionSpec as P

span = 512
chunk = 64
group = 8
width = 128
kv_heads = 4
heads = 32
window = span + chunk
columns = chunk * group
row_axes = ("yh", "x", "c", "yl", "z")
plane_axes = ("yl", "yh", "x", "c")
all_axes = ("z", "yl", "yh", "x", "c")
masked = -1e30
log2e = 1.4426950408889634
factor = width ** -0.5


def place_spans(order_ref, place_ref):
    def put(p, carry):
        place_ref[order_ref[p % 16, p // 16]] = p
        return carry

    lax.fori_loop(0, 32, put, 0)


def expand_kernel(order_ref, meta_ref, pieces_ref, out_ref, place_ref):
    place_spans(order_ref, place_ref)
    z = meta_ref[2]

    def fill(p, carry):
        before = place_ref[jnp.maximum(order_ref[p % 16, p // 16] - 1, 0)]
        own = pieces_ref[p]
        prev = pieces_ref[before]
        for j in range(8):
            @pl.when(j > z)
            def _():
                out_ref[j, p] = own

            @pl.when(j <= z)
            def _():
                out_ref[j, p] = prev
        return carry

    lax.fori_loop(0, 32, fill, 0)


def reduce_kernel(order_ref, meta_ref, parts_ref, out_ref, place_ref, own_ref, prev_ref):
    place_spans(order_ref, place_ref)
    z = meta_ref[2]

    def add(p, carry):
        own = jnp.zeros((16, width), jnp.float32)
        prev = jnp.zeros((16, width), jnp.float32)
        for j in range(8):
            part = parts_ref[j, p].astype(jnp.float32)
            own = own + jnp.where(j > z, part, 0.0)
            prev = prev + jnp.where(j > z, 0.0, part)
        own_ref[p] = own
        prev_ref[p] = prev
        return carry

    lax.fori_loop(0, 32, add, 0)

    def merge(p, carry):
        here = order_ref[p % 16, p // 16]
        after = place_ref[jnp.minimum(here + 1, 31)]
        out_ref[p] = own_ref[p] + jnp.where(here < 31, prev_ref[after], 0.0)
        return carry

    lax.fori_loop(0, 32, merge, 0)


def attention_kernel(
    order_ref,
    lengths_ref,
    meta_ref,
    query_ref,
    grad_ref,
    out_ref,
    window_ref,
    own_ref,
    query_grad_ref,
    window_grad_ref,
    own_grad_ref,
    bias_ref,
    query_acc_ref,
):
    place = meta_ref[2]
    current = order_ref[meta_ref[0], meta_ref[1]]
    base = (current - 1) * span
    token = lax.shift_right_logical(
        lax.broadcasted_iota(jnp.int32, (1, columns), 1), 3
    )
    last = span + place * chunk + token

    def doc(i, carry):
        end, low = carry
        end = end + lengths_ref[i]
        return end, jnp.where(end <= last, jnp.maximum(low, end), low)

    first_end = jnp.int32(0) - base
    low_start = jnp.zeros((1, columns), jnp.int32) + first_end
    _, low = lax.fori_loop(0, 63, doc, (first_end, low_start))
    row = lax.broadcasted_iota(jnp.int32, (window, columns), 0)
    key_at = jnp.where(
        row >= span,
        row + place * chunk,
        jnp.where(lax.shift_right_logical(row, 6) >= place, row, row + span),
    )
    allowed = (key_at <= last) & (key_at >= low)
    bias_ref[...] = jnp.where(allowed, 0.0, masked)
    ones = jnp.ones((8, width), jnp.bfloat16)

    def nt(a, b):
        return lax.dot_general(
            a, b, (((1,), (1,)), ((), ())), preferred_element_type=jnp.float32
        )

    for h in range(kv_heads):
        cut = slice(h * group, (h + 1) * group)
        query = query_ref[...].astype(jnp.float32)[:, cut].reshape(columns, width)
        grad = grad_ref[...].astype(jnp.float32)[:, cut].reshape(columns, width)
        out = out_ref[...].astype(jnp.float32)[:, cut].reshape(columns, width)
        product = grad * out
        high = product.astype(jnp.bfloat16)
        rest = (product - high.astype(jnp.float32)).astype(jnp.bfloat16)
        delta = (nt(ones, high) + nt(ones, rest))[0:1]
        query = query.astype(jnp.bfloat16)
        grad = grad.astype(jnp.bfloat16)
        key = jnp.concatenate(
            [window_ref[:, h, 0].reshape(span, width), own_ref[h, 0]], axis=0
        )
        value = jnp.concatenate(
            [window_ref[:, h, 1].reshape(span, width), own_ref[h, 1]], axis=0
        )
        scores = nt(key, query) * (factor * log2e) + bias_ref[...]
        top = jnp.max(scores, axis=0, keepdims=True)
        exps = jnp.exp2(scores - top)
        total = jnp.sum(exps, axis=0, keepdims=True)
        probs = exps * (1.0 / total)
        grad_scores = (probs * (nt(value, grad) - delta)).astype(jnp.bfloat16)
        value_part = jnp.dot(
            probs.astype(jnp.bfloat16), grad, preferred_element_type=jnp.float32
        )
        key_part = (
            jnp.dot(grad_scores, query, preferred_element_type=jnp.float32) * factor
        )
        query_part = lax.dot_general(
            key, grad_scores, (((0,), (0,)), ((), ())), preferred_element_type=jnp.float32
        )
        query_acc_ref[:, cut] = (jnp.transpose(query_part) * factor).reshape(
            chunk, group, width
        )
        window_grad_ref[:, h, 0] = key_part[:span].astype(jnp.bfloat16).reshape(8, chunk, width)
        window_grad_ref[:, h, 1] = value_part[:span].astype(jnp.bfloat16).reshape(8, chunk, width)
        own_grad_ref[h, 0] = key_part[span:]
        own_grad_ref[h, 1] = value_part[span:]
    query_grad_ref[...] = query_acc_ref[...].astype(jnp.bfloat16)


vmem = pl.BlockSpec(memory_space=pltpu.VMEM)
smem = pl.BlockSpec(memory_space=pltpu.SMEM)


def shards(queries, keys, values, attention_out, out_grad, span_order, doc_lengths):
    query_index = (lax.axis_index("yh") * 4 + lax.axis_index("x")) * 2 + lax.axis_index("c")
    meta = jnp.stack([query_index, lax.axis_index("yl"), lax.axis_index("z")]).astype(jnp.int32)
    own = jnp.transpose(jnp.stack([keys, values], axis=2), (1, 2, 0, 3))
    pieces = lax.all_to_all(
        own.reshape(32, 16, width), plane_axes, split_axis=0, concat_axis=0, tiled=True
    )
    spread = pl.pallas_call(
        expand_kernel,
        out_shape=jax.ShapeDtypeStruct((8, 32, 16, width), jnp.bfloat16),
        in_specs=[smem, smem, vmem],
        out_specs=vmem,
        scratch_shapes=[pltpu.SMEM((32,), jnp.int32)],
    )(span_order, meta, pieces)
    around = lax.all_to_all(
        spread.reshape(256, 16, width), all_axes, split_axis=0, concat_axis=0, tiled=True
    )
    query_grad, window_grad, own_grad = pl.pallas_call(
        attention_kernel,
        out_shape=(
            jax.ShapeDtypeStruct((chunk, heads, width), jnp.bfloat16),
            jax.ShapeDtypeStruct((8, kv_heads, 2, chunk, width), jnp.bfloat16),
            jax.ShapeDtypeStruct((kv_heads, 2, chunk, width), jnp.float32),
        ),
        in_specs=[smem, smem, smem, vmem, vmem, vmem, vmem, vmem],
        out_specs=(vmem, vmem, vmem),
        scratch_shapes=[
            pltpu.VMEM((window, columns), jnp.float32),
            pltpu.VMEM((chunk, heads, width), jnp.float32),
        ],
    )(
        span_order,
        doc_lengths,
        meta,
        queries,
        out_grad,
        attention_out,
        around.reshape(8, kv_heads, 2, chunk, width),
        own,
    )
    parts = lax.all_to_all(
        window_grad.reshape(256, 16, width), all_axes, split_axis=0, concat_axis=0, tiled=True
    )
    sums = pl.pallas_call(
        reduce_kernel,
        out_shape=jax.ShapeDtypeStruct((32, 16, width), jnp.float32),
        in_specs=[smem, smem, vmem],
        out_specs=vmem,
        scratch_shapes=[
            pltpu.SMEM((32,), jnp.int32),
            pltpu.VMEM((32, 16, width), jnp.float32),
            pltpu.VMEM((32, 16, width), jnp.float32),
        ],
    )(span_order, meta, parts.reshape(8, 32, 16, width))
    back = lax.all_to_all(sums, plane_axes, split_axis=0, concat_axis=0, tiled=True)
    both = own_grad + back.reshape(kv_heads, 2, chunk, width)
    both = jnp.transpose(both, (1, 2, 0, 3)).astype(jnp.bfloat16)
    return query_grad, both[0], both[1]


def solution(mesh):
    fine = Mesh(mesh.devices.reshape(2, 8, 2, 4, 2), ("yl", "z", "yh", "x", "c"))
    rows = P(row_axes, None, None)
    return jax.shard_map(
        shards,
        mesh=fine,
        in_specs=(rows, rows, rows, rows, rows, P(), P()),
        out_specs=(rows, rows, rows),
        check_vma=False,
    )
```

```python
import jax
import jax.numpy as jnp
from jax import lax
from jax.experimental import pallas as pl
from jax.experimental.pallas import tpu as pltpu
from jax.sharding import Mesh, PartitionSpec as P


span = 512
chunk = 64
group = 8
width = 128
kv_heads = 4
share = 2
local_kv = kv_heads // share
local_heads = local_kv * group
piece = 16 // share
window = span + share * chunk
columns = chunk * group
row_axes = ("yh", "x", "c", "yl", "z")
plane_axes = ("yl", "yh", "x", "c")
all_axes = ("z", "yl", "yh", "x", "c")
masked = -1e30
log2e = 1.4426950408889634
factor = width ** -0.5


def nt(a, b):
    return lax.dot_general(
        a, b, (((1,), (1,)), ((), ())), preferred_element_type=jnp.float32
    )


def place_spans(order_ref, place_ref):
    for p in range(32):
        place_ref[order_ref[p % 16, p // 16]] = p


def later(j, z):
    return j // share > lax.div(z, share)


def expand_kernel(order_ref, meta_ref, pieces_ref, out_ref, place_ref, prev_ref):
    place_spans(order_ref, place_ref)
    z = meta_ref[2]
    for p in range(32):
        before = place_ref[jnp.maximum(order_ref[p % 16, p // 16] - 1, 0)]
        prev_ref[p] = pieces_ref[before]
    for j in range(8):
        @pl.when(later(j, z))
        def _():
            out_ref[j] = pieces_ref[:, j % share]

        @pl.when(jnp.logical_not(later(j, z)))
        def _():
            out_ref[j] = prev_ref[:, j % share]


def reduce_kernel(order_ref, meta_ref, parts_ref, out_ref, place_ref, own_ref, prev_ref):
    place_spans(order_ref, place_ref)
    z = meta_ref[2]
    for e in range(share):
        own = jnp.zeros((32, piece, width), jnp.float32)
        prev = jnp.zeros((32, piece, width), jnp.float32)
        for j in range(e, 8, share):
            part = parts_ref[j].astype(jnp.float32)
            own = own + jnp.where(later(j, z), part, 0.0)
            prev = prev + jnp.where(later(j, z), 0.0, part)
        own_ref[:, e] = own
        prev_ref[:, e] = prev
    for p in range(32):
        here = order_ref[p % 16, p // 16]
        after = place_ref[jnp.minimum(here + 1, 31)]
        total = own_ref[p] + jnp.where(here < 31, prev_ref[after], 0.0)
        out_ref[p] = total.astype(out_ref.dtype)


def delta_kernel(grad_ref, out_ref, delta_ref):
    ones = jnp.ones((8, width), jnp.bfloat16)
    for h in range(kv_heads):
        cut = slice(h * group, (h + 1) * group)
        grad = grad_ref[...].astype(jnp.float32)[:, cut].reshape(columns, width)
        out = out_ref[...].astype(jnp.float32)[:, cut].reshape(columns, width)
        product = grad * out
        high = product.astype(jnp.bfloat16)
        rest = (product - high.astype(jnp.float32)).astype(jnp.bfloat16)
        delta_ref[h : h + 1] = (nt(ones, high) + nt(ones, rest))[0:1]


def attention_kernel(*refs):
    order_ref, lengths_ref, meta_ref = refs[:3]
    query_refs = refs[3 : 3 + share]
    grad_refs = refs[3 + share : 3 + 2 * share]
    delta_refs = refs[3 + 2 * share : 3 + 3 * share]
    own_refs = refs[3 + 3 * share : 3 + 4 * share]
    window_ref = refs[3 + 4 * share]
    results = refs[4 + 4 * share :]
    query_grad_refs = results[:share]
    own_grad_refs = results[share : 2 * share]
    window_grad_ref, bias_ref, key_acc_ref, value_acc_ref, query_acc_ref = results[2 * share :]
    place = meta_ref[2]
    current = order_ref[meta_ref[0], meta_ref[1]]
    base = (current - 1) * span
    token = lax.shift_right_logical(
        lax.broadcasted_iota(jnp.int32, (1, columns), 1), 3
    )
    lasts = [span + (place ^ b) * chunk + token for b in range(share)]

    def doc(i, carry):
        end, lows = carry
        end = end + lengths_ref[i]
        return end, tuple(
            jnp.where(end <= last, jnp.maximum(low, end), low)
            for low, last in zip(lows, lasts)
        )

    first_end = jnp.int32(0) - base
    low_start = jnp.zeros((1, columns), jnp.int32) + first_end
    _, lows = lax.fori_loop(0, 63, doc, (first_end, (low_start,) * share))
    row = lax.broadcasted_iota(jnp.int32, (window, columns), 0)
    stretch = lax.shift_right_logical(row, 6)
    key_at = jnp.where(
        lax.div(stretch, share) >= lax.div(place, share), row, row + span
    )
    for b in range(share):
        key_at = jnp.where(
            stretch == 8 + b, row - b * chunk + (place ^ b) * chunk, key_at
        )
    for b in range(share):
        allowed = (key_at <= lasts[b]) & (key_at >= lows[b])
        bias_ref[...] = jnp.where(allowed, 0.0, masked)
        for h in range(local_kv):
            cut = slice(h * group, (h + 1) * group)
            query = query_refs[b][...].astype(jnp.float32)[:, cut].reshape(columns, width)
            grad = grad_refs[b][...].astype(jnp.float32)[:, cut].reshape(columns, width)
            query = query.astype(jnp.bfloat16)
            grad = grad.astype(jnp.bfloat16)
            delta = delta_refs[b][h : h + 1]
            key = jnp.concatenate(
                [window_ref[:, h, 0].reshape(span, width)] + [own[h, 0] for own in own_refs],
                axis=0,
            )
            value = jnp.concatenate(
                [window_ref[:, h, 1].reshape(span, width)] + [own[h, 1] for own in own_refs],
                axis=0,
            )
            scores = nt(key, query) * (factor * log2e) + bias_ref[...]
            top = jnp.max(scores, axis=0, keepdims=True)
            exps = jnp.exp2(scores - top)
            total = jnp.sum(exps, axis=0, keepdims=True)
            probs = exps * (1.0 / total)
            grad_scores = (probs * (nt(value, grad) - delta)).astype(jnp.bfloat16)
            value_part = jnp.dot(
                probs.astype(jnp.bfloat16), grad, preferred_element_type=jnp.float32
            )
            key_part = jnp.dot(grad_scores, query, preferred_element_type=jnp.float32)
            query_part = lax.dot_general(
                key, grad_scores, (((0,), (0,)), ((), ())), preferred_element_type=jnp.float32
            )
            query_acc_ref[:, cut] = (jnp.transpose(query_part) * factor).reshape(
                chunk, group, width
            )
            if b > 0:
                key_part = key_part + key_acc_ref[h]
                value_part = value_part + value_acc_ref[h]
            if b < share - 1:
                key_acc_ref[h] = key_part
                value_acc_ref[h] = value_part
            else:
                key_part = key_part * factor
                window_grad_ref[:, h, 0] = key_part[:span].astype(jnp.bfloat16).reshape(8, chunk, width)
                window_grad_ref[:, h, 1] = value_part[:span].astype(jnp.bfloat16).reshape(8, chunk, width)
                for k in range(share):
                    at = slice(span + k * chunk, span + (k + 1) * chunk)
                    kind = own_grad_refs[k].dtype
                    own_grad_refs[k][h, 0] = key_part[at].astype(kind)
                    own_grad_refs[k][h, 1] = value_part[at].astype(kind)
        query_grad_refs[b][...] = query_acc_ref[...].astype(jnp.bfloat16)


vmem = pl.BlockSpec(memory_space=pltpu.VMEM)
smem = pl.BlockSpec(memory_space=pltpu.SMEM)
low = jnp.bfloat16


def trade(array, b):
    return lax.ppermute(array, "z", [(i, i ^ b) for i in range(8)])


def route(array, axes):
    return lax.all_to_all(array, axes, split_axis=0, concat_axis=0, tiled=True)


def shards(queries, keys, values, attention_out, out_grad, span_order, doc_lengths):
    z = lax.axis_index("z")
    mine = lax.rem(z, share)
    query_index = (lax.axis_index("yh") * 4 + lax.axis_index("x")) * 2 + lax.axis_index("c")
    meta = jnp.stack([query_index, lax.axis_index("yl"), z]).astype(jnp.int32)
    own = jnp.transpose(jnp.stack([keys, values], axis=2), (1, 2, 0, 3))
    own = own.reshape(share, 32, piece, width)
    pieces = route(jnp.transpose(own, (1, 0, 2, 3)), plane_axes)
    own = own.reshape(share, local_kv, 2, chunk, width)
    delta = pl.pallas_call(
        delta_kernel,
        out_shape=jax.ShapeDtypeStruct((kv_heads, columns), jnp.float32),
        in_specs=[vmem, vmem],
        out_specs=vmem,
    )(out_grad, attention_out).reshape(share, local_kv, columns)

    def gathered(array, axis, count):
        parts = []
        for b in range(share):
            part = lax.dynamic_slice_in_dim(array, (mine ^ b) * count, count, axis)
            parts.append(trade(part, b) if b else part)
        return parts

    query_parts = gathered(queries, 1, local_heads)
    grad_parts = gathered(out_grad, 1, local_heads)
    delta_parts = [d.reshape(local_kv, columns) for d in gathered(delta, 0, 1)]
    own_parts = [o.reshape(local_kv, 2, chunk, width) for o in gathered(own, 0, 1)]

    spread = pl.pallas_call(
        expand_kernel,
        out_shape=jax.ShapeDtypeStruct((8, 32, piece, width), low),
        in_specs=[smem, smem, vmem],
        out_specs=vmem,
        scratch_shapes=[
            pltpu.SMEM((32,), jnp.int32),
            pltpu.VMEM((32, share, piece, width), low),
        ],
    )(span_order, meta, pieces)
    around = route(spread.reshape(256, piece, width), all_axes)
    results = pl.pallas_call(
        attention_kernel,
        out_shape=tuple(
            [jax.ShapeDtypeStruct((chunk, local_heads, width), low)] * share
            + [jax.ShapeDtypeStruct((local_kv, 2, chunk, width), jnp.float32)]
            + [jax.ShapeDtypeStruct((local_kv, 2, chunk, width), low)] * (share - 1)
            + [jax.ShapeDtypeStruct((8, local_kv, 2, chunk, width), low)]
        ),
        in_specs=[smem] * 3 + [vmem] * (4 * share + 1),
        out_specs=tuple([vmem] * (2 * share + 1)),
        scratch_shapes=[
            pltpu.VMEM((window, columns), jnp.float32),
            pltpu.VMEM((local_kv, window, width), jnp.float32),
            pltpu.VMEM((local_kv, window, width), jnp.float32),
            pltpu.VMEM((chunk, local_heads, width), jnp.float32),
        ],
    )(
        span_order,
        doc_lengths,
        meta,
        *query_parts,
        *grad_parts,
        *delta_parts,
        *own_parts,
        around.reshape(8, local_kv, 2, chunk, width),
    )
    query_grads = list(results[:share])
    own_grads = list(results[share : 2 * share])
    parts = route(results[-1].reshape(256, piece, width), all_axes)
    for b in range(1, share):
        query_grads[b] = trade(query_grads[b], b)
        own_grads[b] = trade(own_grads[b], b)
    sums = pl.pallas_call(
        reduce_kernel,
        out_shape=jax.ShapeDtypeStruct((32, share, piece, width), low),
        in_specs=[smem, smem, vmem],
        out_specs=vmem,
        scratch_shapes=[
            pltpu.SMEM((32,), jnp.int32),
            pltpu.VMEM((32, share, piece, width), jnp.float32),
            pltpu.VMEM((32, share, piece, width), jnp.float32),
        ],
    )(span_order, meta, parts.reshape(8, 32, piece, width))
    back = route(sums, plane_axes)
    back = jnp.transpose(back, (1, 0, 2, 3)).reshape(share, local_kv, 2, chunk, width)

    def arranged(members):
        columns_of = []
        for e in range(share):
            chosen = members[0]
            for b in range(1, share):
                chosen = jnp.where((mine ^ b) == e, members[b], chosen)
            columns_of.append(chosen)
        return columns_of

    query_grad = jnp.concatenate(arranged(query_grads), axis=1)
    both = jnp.stack(arranged([m.astype(jnp.float32) for m in own_grads])) + back
    both = both.reshape(kv_heads, 2, chunk, width)
    both = jnp.transpose(both, (1, 2, 0, 3)).astype(low)
    return query_grad, both[0], both[1]


def solution(mesh):
    fine = Mesh(mesh.devices.reshape(2, 8, 2, 4, 2), ("yl", "z", "yh", "x", "c"))
    rows = P(row_axes, None, None)
    return jax.shard_map(
        shards,
        mesh=fine,
        in_specs=(rows, rows, rows, rows, rows, P(), P()),
        out_specs=(rows, rows, rows),
        check_vma=False,
    )
```

```python
import jax
import jax.numpy as jnp
from jax import lax
from jax.experimental import pallas as pl
from jax.experimental.pallas import tpu as pltpu
from jax.sharding import Mesh, PartitionSpec as P


span = 512
chunk = 64
group = 8
width = 128
kv_heads = 4
heads = 32
share = 2
local_kv = kv_heads // share
piece = 16 // share
window = span + share * chunk
columns = chunk * group
row_axes = ("yh", "x", "c", "yl", "z")
plane_axes = ("yl", "yh", "x", "c")
all_axes = ("yl", "yh", "x", "c", "z")
masked = -1e30
log2e = 1.4426950408889634
factor = width ** -0.5


def nt(a, b):
    return lax.dot_general(
        a, b, (((1,), (1,)), ((), ())), preferred_element_type=jnp.float32
    )


def place_spans(order_ref, place_ref):
    for p in range(32):
        place_ref[order_ref[p % 16, p // 16]] = p


def later(j, z):
    return j // share > lax.div(z, share)


def expand_kernel(order_ref, meta_ref, pieces_ref, out_ref, place_ref, prev_ref):
    place_spans(order_ref, place_ref)
    z = meta_ref[2]
    for p in range(32):
        before = place_ref[jnp.maximum(order_ref[p % 16, p // 16] - 1, 0)]
        prev_ref[p] = pieces_ref[before]
    for j in range(8):
        @pl.when(later(j, z))
        def _():
            out_ref[:, j] = pieces_ref[:, j % share]

        @pl.when(jnp.logical_not(later(j, z)))
        def _():
            out_ref[:, j] = prev_ref[:, j % share]


def reduce_kernel(order_ref, meta_ref, parts_ref, out_ref, place_ref, own_ref, prev_ref):
    place_spans(order_ref, place_ref)
    z = meta_ref[2]
    for e in range(share):
        own = jnp.zeros((32, piece, width), jnp.float32)
        prev = jnp.zeros((32, piece, width), jnp.float32)
        for j in range(e, 8, share):
            part = parts_ref[:, j].astype(jnp.float32)
            own = own + jnp.where(later(j, z), part, 0.0)
            prev = prev + jnp.where(later(j, z), 0.0, part)
        own_ref[:, e] = own
        prev_ref[:, e] = prev
    for p in range(32):
        here = order_ref[p % 16, p // 16]
        after = place_ref[jnp.minimum(here + 1, 31)]
        total = own_ref[p] + jnp.where(here < 31, prev_ref[after], 0.0)
        out_ref[p] = total.astype(out_ref.dtype)


def delta_kernel(grad_ref, out_ref, delta_ref):
    ones = jnp.ones((8, width), jnp.bfloat16)
    for h in range(kv_heads):
        cut = slice(h * group, (h + 1) * group)
        grad = grad_ref[...].astype(jnp.float32)[:, cut].reshape(columns, width)
        out = out_ref[...].astype(jnp.float32)[:, cut].reshape(columns, width)
        product = grad * out
        high = product.astype(jnp.bfloat16)
        rest = (product - high.astype(jnp.float32)).astype(jnp.bfloat16)
        delta_ref[h : h + 1] = (nt(ones, high) + nt(ones, rest))[0:1]


def attention_kernel(*refs):
    order_ref, lengths_ref, meta_ref = refs[:3]
    message_refs = refs[3 : 3 + share]
    delta_refs = refs[3 + share : 3 + 2 * share]
    window_ref = refs[3 + 2 * share]
    results = refs[4 + 2 * share :]
    result_refs = results[:share]
    own_grad_ref, window_grad_ref, bias_ref, key_acc_ref, value_acc_ref = results[share:]
    place = meta_ref[2]
    current = order_ref[meta_ref[0], meta_ref[1]]
    base = (current - 1) * span
    token = lax.shift_right_logical(
        lax.broadcasted_iota(jnp.int32, (1, columns), 1), 3
    )
    lasts = [span + (place ^ b) * chunk + token for b in range(share)]

    def doc(i, carry):
        end, lows = carry
        end = end + lengths_ref[i]
        return end, tuple(
            jnp.where(end <= last, jnp.maximum(low, end), low)
            for low, last in zip(lows, lasts)
        )

    first_end = jnp.int32(0) - base
    low_start = jnp.zeros((1, columns), jnp.int32) + first_end
    _, lows = lax.fori_loop(0, 63, doc, (first_end, (low_start,) * share))
    row = lax.broadcasted_iota(jnp.int32, (window, columns), 0)
    stretch = lax.shift_right_logical(row, 6)
    source = lax.div(row, piece) & 7
    inside = lax.div(row, 8 * piece) * piece + (row & (piece - 1))
    key_at = source * chunk + inside
    key_at = jnp.where(
        lax.div(source, share) >= lax.div(place, share), key_at, key_at + span
    )
    for b in range(share):
        key_at = jnp.where(
            stretch == 8 + b, row - b * chunk + (place ^ b) * chunk, key_at
        )

    def own_rows(b, h, kind):
        start = local_kv * 2 * columns + (h * 2 + kind) * chunk
        return message_refs[b][start : start + chunk]

    for b in range(share):
        allowed = (key_at <= lasts[b]) & (key_at >= lows[b])
        bias_ref[...] = jnp.where(allowed, 0.0, masked)
        for h in range(local_kv):
            query = message_refs[b][h * columns : (h + 1) * columns]
            grad = message_refs[b][(local_kv + h) * columns : (local_kv + h + 1) * columns]
            delta = delta_refs[b][h : h + 1]
            key = jnp.concatenate(
                [window_ref[h, 0]]
                + [own_rows(k, h, 0) for k in range(share)],
                axis=0,
            )
            value = jnp.concatenate(
                [window_ref[h, 1]]
                + [own_rows(k, h, 1) for k in range(share)],
                axis=0,
            )
            scores = nt(key, query) * (factor * log2e) + bias_ref[...]
            top = jnp.max(scores, axis=0, keepdims=True)
            exps = jnp.exp2(scores - top)
            total = jnp.sum(exps, axis=0, keepdims=True)
            probs = exps * (1.0 / total)
            grad_scores = (probs * (nt(value, grad) - delta)).astype(low)
            value_part = jnp.dot(
                probs.astype(low), grad, preferred_element_type=jnp.float32
            )
            key_part = jnp.dot(grad_scores, query, preferred_element_type=jnp.float32)
            query_part = lax.dot_general(
                key, grad_scores, (((0,), (0,)), ((), ())), preferred_element_type=jnp.float32
            )
            result_refs[b][h * columns : (h + 1) * columns] = (
                jnp.transpose(query_part) * factor
            ).astype(low)
            if b > 0:
                key_part = key_part + key_acc_ref[h]
                value_part = value_part + value_acc_ref[h]
            if b < share - 1:
                key_acc_ref[h] = key_part
                value_acc_ref[h] = value_part
            else:
                key_part = key_part * factor
                window_grad_ref[h, 0] = key_part[:span].astype(low)
                window_grad_ref[h, 1] = value_part[:span].astype(low)
                for k in range(share):
                    at = slice(span + k * chunk, span + (k + 1) * chunk)
                    for kind, part in enumerate((key_part, value_part)):
                        start = (h * 2 + kind) * chunk
                        if k == 0:
                            own_grad_ref[start : start + chunk] = part[at]
                        else:
                            start = start + local_kv * columns
                            result_refs[k][start : start + chunk] = part[at].astype(low)


vmem = pl.BlockSpec(memory_space=pltpu.VMEM)
smem = pl.BlockSpec(memory_space=pltpu.SMEM)
low = jnp.bfloat16


def trade(array, b):
    return lax.ppermute(array, "z", [(i, i ^ b) for i in range(8)])


def route(array, axes):
    return lax.all_to_all(array, axes, split_axis=0, concat_axis=0, tiled=True)


def shards(queries, keys, values, attention_out, out_grad, span_order, doc_lengths):
    z = lax.axis_index("z")
    mine = lax.rem(z, share)
    query_index = (lax.axis_index("yh") * 4 + lax.axis_index("x")) * 2 + lax.axis_index("c")
    meta = jnp.stack([query_index, lax.axis_index("yl"), z]).astype(jnp.int32)
    own = jnp.stack([jnp.transpose(keys, (1, 0, 2)), jnp.transpose(values, (1, 0, 2))], axis=1)
    own = own.reshape(share, 32, piece, width)
    pieces = route(jnp.transpose(own, (1, 0, 2, 3)), plane_axes)
    delta = pl.pallas_call(
        delta_kernel,
        out_shape=jax.ShapeDtypeStruct((kv_heads, columns), jnp.float32),
        in_specs=[vmem, vmem],
        out_specs=vmem,
    )(out_grad, attention_out).reshape(share, local_kv, columns)

    def per_share(array):
        array = array.reshape(chunk, share, local_kv, group, width)
        return jnp.transpose(array, (1, 2, 0, 3, 4)).reshape(share, local_kv * columns, width)

    whole = jnp.concatenate(
        [per_share(queries), per_share(out_grad), own.reshape(share, -1, width)], axis=1
    )
    messages = []
    deltas = []
    for b in range(share):
        message = lax.dynamic_index_in_dim(whole, mine ^ b, 0, keepdims=False)
        part = lax.dynamic_index_in_dim(delta, mine ^ b, 0, keepdims=False)
        messages.append(trade(message, b) if b else message)
        deltas.append(trade(part, b) if b else part)

    spread = pl.pallas_call(
        expand_kernel,
        out_shape=jax.ShapeDtypeStruct((32, 8, piece, width), low),
        in_specs=[smem, smem, vmem],
        out_specs=vmem,
        scratch_shapes=[
            pltpu.SMEM((32,), jnp.int32),
            pltpu.VMEM((32, share, piece, width), low),
        ],
    )(span_order, meta, pieces)
    around = route(spread.reshape(256, piece, width), all_axes)
    back_rows = local_kv * (columns + 2 * chunk)
    results = pl.pallas_call(
        attention_kernel,
        out_shape=tuple(
            [jax.ShapeDtypeStruct((local_kv * columns, width), low)]
            + [jax.ShapeDtypeStruct((back_rows, width), low)] * (share - 1)
            + [jax.ShapeDtypeStruct((local_kv * 2 * chunk, width), jnp.float32)]
            + [jax.ShapeDtypeStruct((local_kv, 2, span, width), low)]
        ),
        in_specs=[smem] * 3 + [vmem] * (2 * share + 1),
        out_specs=tuple([vmem] * (share + 2)),
        scratch_shapes=[
            pltpu.VMEM((window, columns), jnp.float32),
            pltpu.VMEM((local_kv, window, width), jnp.float32),
            pltpu.VMEM((local_kv, window, width), jnp.float32),
        ],
    )(
        span_order,
        doc_lengths,
        meta,
        *messages,
        *deltas,
        around.reshape(local_kv, 2, span, width),
    )
    parts = route(results[-1].reshape(256, piece, width), all_axes)
    query_grads = [results[0]]
    own_grads = [results[share]]
    for b in range(1, share):
        got = trade(results[b], b)
        query_grads.append(got[: local_kv * columns])
        own_grads.append(got[local_kv * columns :])
    sums = pl.pallas_call(
        reduce_kernel,
        out_shape=jax.ShapeDtypeStruct((32, share, piece, width), low),
        in_specs=[smem, smem, vmem],
        out_specs=vmem,
        scratch_shapes=[
            pltpu.SMEM((32,), jnp.int32),
            pltpu.VMEM((32, share, piece, width), jnp.float32),
            pltpu.VMEM((32, share, piece, width), jnp.float32),
        ],
    )(span_order, meta, parts.reshape(32, 8, piece, width))
    back = route(sums, plane_axes)

    def arranged(members):
        found = []
        for e in range(share):
            chosen = members[0]
            for b in range(1, share):
                chosen = jnp.where((mine ^ b) == e, members[b], chosen)
            found.append(chosen)
        return jnp.stack(found)

    query_grad = arranged(query_grads).reshape(share, local_kv, chunk, group, width)
    query_grad = jnp.transpose(query_grad, (2, 0, 1, 3, 4)).reshape(chunk, heads, width)
    local = arranged([m.astype(jnp.float32) for m in own_grads])
    back, query_grad, local = lax.optimization_barrier((back, query_grad, local))
    back = jnp.transpose(back, (1, 0, 2, 3)).reshape(share, -1, width)
    both = (local + back).reshape(kv_heads, 2, chunk, width)
    both = jnp.transpose(both, (1, 2, 0, 3)).astype(low)
    return query_grad, both[0], both[1]


def solution(mesh):
    fine = Mesh(mesh.devices.reshape(2, 8, 2, 4, 2), ("yl", "z", "yh", "x", "c"))
    rows = P(row_axes, None, None)
    return jax.shard_map(
        shards,
        mesh=fine,
        in_specs=(rows, rows, rows, rows, rows, P(), P()),
        out_specs=(rows, rows, rows),
        check_vma=False,
    )
```

```python
import jax
import jax.numpy as jnp
from jax import lax
from jax.experimental import pallas as pl
from jax.experimental.pallas import tpu as pltpu
from jax.sharding import Mesh, PartitionSpec as P


span = 512
chunk = 64
group = 8
width = 128
kv_heads = 4
heads = 32
share = 2
local_kv = kv_heads // share
piece = 16 // share
window = span + share * chunk
columns = chunk * group
row_axes = ("yh", "x", "c", "yl", "z")
plane_axes = ("yl", "yh", "x", "c")
all_axes = ("yl", "yh", "x", "c", "z")
masked = -1e30
log2e = 1.4426950408889634
factor = width ** -0.5


def nt(a, b):
    return lax.dot_general(
        a, b, (((1,), (1,)), ((), ())), preferred_element_type=jnp.float32
    )


def place_spans(order_ref, place_ref):
    for p in range(32):
        place_ref[order_ref[p % 16, p // 16]] = p


def later(j, z):
    return j // share > lax.div(z, share)


def expand_kernel(order_ref, meta_ref, pieces_ref, out_ref, place_ref, prev_ref):
    place_spans(order_ref, place_ref)
    z = meta_ref[2]
    for p in range(32):
        before = place_ref[jnp.maximum(order_ref[p % 16, p // 16] - 1, 0)]
        prev_ref[p] = pieces_ref[before]
    for j in range(8):
        @pl.when(later(j, z))
        def _():
            out_ref[:, j] = pieces_ref[:, j % share]

        @pl.when(jnp.logical_not(later(j, z)))
        def _():
            out_ref[:, j] = prev_ref[:, j % share]


def reduce_kernel(order_ref, meta_ref, parts_ref, out_ref, place_ref, own_ref, prev_ref):
    place_spans(order_ref, place_ref)
    z = meta_ref[2]
    for e in range(share):
        own = jnp.zeros((32, piece, width), jnp.float32)
        prev = jnp.zeros((32, piece, width), jnp.float32)
        for j in range(e, 8, share):
            part = parts_ref[:, j].astype(jnp.float32)
            own = own + jnp.where(later(j, z), part, 0.0)
            prev = prev + jnp.where(later(j, z), 0.0, part)
        own_ref[:, e] = own
        prev_ref[:, e] = prev
    for p in range(32):
        here = order_ref[p % 16, p // 16]
        after = place_ref[jnp.minimum(here + 1, 31)]
        total = own_ref[p] + jnp.where(here < 31, prev_ref[after], 0.0)
        out_ref[p] = total.astype(out_ref.dtype)


def delta_kernel(grad_ref, out_ref, delta_ref):
    ones = jnp.ones((8, width), jnp.bfloat16)
    for h in range(kv_heads):
        cut = slice(h * group, (h + 1) * group)
        grad = grad_ref[...].astype(jnp.float32)[:, cut].reshape(columns, width)
        out = out_ref[...].astype(jnp.float32)[:, cut].reshape(columns, width)
        product = grad * out
        high = product.astype(jnp.bfloat16)
        rest = (product - high.astype(jnp.float32)).astype(jnp.bfloat16)
        delta_ref[h : h + 1] = (nt(ones, high) + nt(ones, rest))[0:1]


def attention_kernel(*refs):
    order_ref, lengths_ref, meta_ref = refs[:3]
    message_refs = refs[3 : 3 + share]
    delta_refs = refs[3 + share : 3 + 2 * share]
    window_ref = refs[3 + 2 * share]
    results = refs[4 + 2 * share :]
    result_refs = results[:share]
    own_grad_ref, window_grad_ref, bias_ref, key_acc_ref, value_acc_ref = results[share:]
    place = meta_ref[2]
    current = order_ref[meta_ref[0], meta_ref[1]]
    base = (current - 1) * span
    token = lax.shift_right_logical(
        lax.broadcasted_iota(jnp.int32, (1, columns), 1), 3
    )
    lasts = [span + (place ^ b) * chunk + token for b in range(share)]

    def doc(i, carry):
        end, lows = carry
        end = end + lengths_ref[i]
        return end, tuple(
            jnp.where(end <= last, jnp.maximum(low, end), low)
            for low, last in zip(lows, lasts)
        )

    first_end = jnp.int32(0) - base
    low_start = jnp.zeros((1, columns), jnp.int32) + first_end
    _, lows = lax.fori_loop(0, 63, doc, (first_end, (low_start,) * share))
    row = lax.broadcasted_iota(jnp.int32, (window, columns), 0)
    stretch = lax.shift_right_logical(row, 6)
    source = lax.div(row, piece) & 7
    inside = lax.div(row, 8 * piece) * piece + (row & (piece - 1))
    key_at = source * chunk + inside
    key_at = jnp.where(
        lax.div(source, share) >= lax.div(place, share), key_at, key_at + span
    )
    for b in range(share):
        key_at = jnp.where(
            stretch == 8 + b, row - b * chunk + (place ^ b) * chunk, key_at
        )

    def own_rows(b, h, kind):
        start = local_kv * 2 * columns + (h * 2 + kind) * chunk
        return message_refs[b][start : start + chunk]

    for b in range(share):
        allowed = (key_at <= lasts[b]) & (key_at >= lows[b])
        bias_ref[...] = jnp.where(allowed, 0.0, masked)
        for h in range(local_kv):
            query = message_refs[b][h * columns : (h + 1) * columns]
            grad = message_refs[b][(local_kv + h) * columns : (local_kv + h + 1) * columns]
            delta = delta_refs[b][h : h + 1]
            key = jnp.concatenate(
                [window_ref[h, 0]]
                + [own_rows(k, h, 0) for k in range(share)],
                axis=0,
            )
            value = jnp.concatenate(
                [window_ref[h, 1]]
                + [own_rows(k, h, 1) for k in range(share)],
                axis=0,
            )
            scores = nt(key, query) * (factor * log2e) + bias_ref[...]
            top = jnp.max(scores, axis=0, keepdims=True)
            exps = jnp.exp2(scores - top)
            total = jnp.sum(exps, axis=0, keepdims=True)
            probs = exps * (1.0 / total)
            grad_scores = (probs * (nt(value, grad) - delta)).astype(low)
            value_part = jnp.dot(
                probs.astype(low), grad, preferred_element_type=jnp.float32
            )
            key_part = jnp.dot(grad_scores, query, preferred_element_type=jnp.float32)
            query_part = lax.dot_general(
                key, grad_scores, (((0,), (0,)), ((), ())), preferred_element_type=jnp.float32
            )
            result_refs[b][h * columns : (h + 1) * columns] = (
                jnp.transpose(query_part) * factor
            ).astype(low)
            if b > 0:
                key_part = key_part + key_acc_ref[h]
                value_part = value_part + value_acc_ref[h]
            if b < share - 1:
                key_acc_ref[h] = key_part
                value_acc_ref[h] = value_part
            else:
                key_part = key_part * factor
                window_grad_ref[h, 0] = key_part[:span].astype(low)
                window_grad_ref[h, 1] = value_part[:span].astype(low)
                for k in range(share):
                    at = slice(span + k * chunk, span + (k + 1) * chunk)
                    for kind, part in enumerate((key_part, value_part)):
                        start = (h * 2 + kind) * chunk
                        if k == 0:
                            own_grad_ref[start : start + chunk] = part[at]
                        else:
                            start = start + local_kv * columns
                            result_refs[k][start : start + chunk] = part[at].astype(low)


vmem = pl.BlockSpec(memory_space=pltpu.VMEM)


def near(array):
    return pltpu.with_memory_space_constraint(array, pltpu.VMEM)


smem = pl.BlockSpec(memory_space=pltpu.SMEM)
low = jnp.bfloat16


def trade(array, b):
    return lax.ppermute(array, "z", [(i, i ^ b) for i in range(8)])


def route(array, axes):
    return lax.all_to_all(array, axes, split_axis=0, concat_axis=0, tiled=True)


def shards(queries, keys, values, attention_out, out_grad, span_order, doc_lengths):
    z = lax.axis_index("z")
    mine = lax.rem(z, share)
    query_index = (lax.axis_index("yh") * 4 + lax.axis_index("x")) * 2 + lax.axis_index("c")
    meta = jnp.stack([query_index, lax.axis_index("yl"), z]).astype(jnp.int32)
    own = jnp.stack([jnp.transpose(keys, (1, 0, 2)), jnp.transpose(values, (1, 0, 2))], axis=1)
    own = own.reshape(share, 32, piece, width)
    pieces = route(jnp.transpose(own, (1, 0, 2, 3)), plane_axes)
    delta = pl.pallas_call(
        delta_kernel,
        out_shape=jax.ShapeDtypeStruct((kv_heads, columns), jnp.float32),
        in_specs=[vmem, vmem],
        out_specs=vmem,
    )(out_grad, attention_out).reshape(share, local_kv, columns)

    def per_share(array):
        array = array.reshape(chunk, share, local_kv, group, width)
        return jnp.transpose(array, (1, 2, 0, 3, 4)).reshape(share, local_kv * columns, width)

    whole = jnp.concatenate(
        [per_share(queries), per_share(out_grad), own.reshape(share, -1, width)], axis=1
    )
    messages = []
    deltas = []
    for b in range(share):
        message = lax.dynamic_index_in_dim(whole, mine ^ b, 0, keepdims=False)
        part = lax.dynamic_index_in_dim(delta, mine ^ b, 0, keepdims=False)
        messages.append(trade(message, b) if b else message)
        deltas.append(trade(part, b) if b else part)

    spread = pl.pallas_call(
        expand_kernel,
        out_shape=pltpu.VMEM((32, 8, piece, width), low),
        in_specs=[smem, smem, vmem],
        out_specs=vmem,
        scratch_shapes=[
            pltpu.SMEM((32,), jnp.int32),
            pltpu.VMEM((32, share, piece, width), low),
        ],
    )(span_order, meta, near(pieces))
    around = route(spread.reshape(256, piece, width), all_axes)
    back_rows = local_kv * (columns + 2 * chunk)
    results = pl.pallas_call(
        attention_kernel,
        out_shape=tuple(
            [pltpu.VMEM((local_kv * columns, width), low)]
            + [pltpu.VMEM((back_rows, width), low)] * (share - 1)
            + [pltpu.VMEM((local_kv * 2 * chunk, width), jnp.float32)]
            + [pltpu.VMEM((local_kv, 2, span, width), low)]
        ),
        in_specs=[smem] * 3 + [vmem] * (2 * share + 1),
        out_specs=tuple([vmem] * (share + 2)),
        scratch_shapes=[
            pltpu.VMEM((window, columns), jnp.float32),
            pltpu.VMEM((local_kv, window, width), jnp.float32),
            pltpu.VMEM((local_kv, window, width), jnp.float32),
        ],
    )(
        span_order,
        doc_lengths,
        meta,
        *[near(m) for m in messages],
        *deltas,
        near(around.reshape(local_kv, 2, span, width)),
    )
    parts = route(results[-1].reshape(256, piece, width), all_axes)
    query_grads = [results[0]]
    own_grads = [results[share]]
    for b in range(1, share):
        got = trade(results[b], b)
        query_grads.append(got[: local_kv * columns])
        own_grads.append(got[local_kv * columns :])
    sums = pl.pallas_call(
        reduce_kernel,
        out_shape=pltpu.VMEM((32, share, piece, width), low),
        in_specs=[smem, smem, vmem],
        out_specs=vmem,
        scratch_shapes=[
            pltpu.SMEM((32,), jnp.int32),
            pltpu.VMEM((32, share, piece, width), jnp.float32),
            pltpu.VMEM((32, share, piece, width), jnp.float32),
        ],
    )(span_order, meta, near(parts.reshape(32, 8, piece, width)))
    back = route(sums, plane_axes)

    def arranged(members):
        found = []
        for e in range(share):
            chosen = members[0]
            for b in range(1, share):
                chosen = jnp.where((mine ^ b) == e, members[b], chosen)
            found.append(chosen)
        return jnp.stack(found)

    query_grad = arranged(query_grads).reshape(share, local_kv, chunk, group, width)
    query_grad = jnp.transpose(query_grad, (2, 0, 1, 3, 4)).reshape(chunk, heads, width)
    local = arranged([m.astype(jnp.float32) for m in own_grads])
    back, query_grad, local = lax.optimization_barrier((back, query_grad, local))
    back = jnp.transpose(back, (1, 0, 2, 3)).reshape(share, -1, width)
    both = (local + back).reshape(kv_heads, 2, chunk, width)
    both = jnp.transpose(both, (1, 2, 0, 3)).astype(low)
    return query_grad, both[0], both[1]


def solution(mesh):
    fine = Mesh(mesh.devices.reshape(2, 8, 2, 4, 2), ("yl", "z", "yh", "x", "c"))
    rows = P(row_axes, None, None)
    return jax.shard_map(
        shards,
        mesh=fine,
        in_specs=(rows, rows, rows, rows, rows, P(), P()),
        out_specs=(rows, rows, rows),
        check_vma=False,
    )
```

```python
import jax
import jax.numpy as jnp
from jax import lax
from jax.experimental import pallas as pl
from jax.experimental.pallas import tpu as pltpu
from jax.sharding import Mesh, PartitionSpec as P


span = 512
chunk = 64
group = 8
width = 128
kv_heads = 4
heads = 32
share = 2
local_kv = kv_heads // share
piece = 16 // share
window = span + share * chunk
columns = chunk * group
merged = 2
row_axes = ("yh", "x", "c", "yl", "z")
plane_axes = ("yl", "yh", "x", "c")
all_axes = ("yl", "yh", "x", "c", "z")
masked = -1e30
log2e = 1.4426950408889634
factor = width ** -0.5


def nt(a, b):
    return lax.dot_general(
        a, b, (((1,), (1,)), ((), ())), preferred_element_type=jnp.float32
    )


def expand_kernel(table_ref, pieces_ref, out_ref, plan_ref, prev_ref):
    pltpu.sync_copy(table_ref, plan_ref)
    z = plan_ref[0, 64]
    for p in range(32):
        prev_ref[p] = pieces_ref[plan_ref[0, p]]
    for j in range(8):
        later = j // share > lax.div(z, share)

        @pl.when(later)
        def _():
            out_ref[:, j] = pieces_ref[:, j % share]

        @pl.when(jnp.logical_not(later))
        def _():
            out_ref[:, j] = prev_ref[:, j % share]


def reduce_kernel(table_ref, parts_ref, out_ref, plan_ref, own_ref, prev_ref):
    pltpu.sync_copy(table_ref, plan_ref)
    z = plan_ref[0, 64]
    prev_ref[32] = jnp.zeros((share, piece, width), jnp.float32)
    for e in range(share):
        own = jnp.zeros((32, piece, width), jnp.float32)
        prev = jnp.zeros((32, piece, width), jnp.float32)
        for j in range(e, 8, share):
            later = j // share > lax.div(z, share)
            part = parts_ref[:, j].astype(jnp.float32)
            own = own + jnp.where(later, part, 0.0)
            prev = prev + jnp.where(later, 0.0, part)
        own_ref[:, e] = own
        prev_ref[:32, e] = prev
    for p in range(32):
        out_ref[p] = (own_ref[p] + prev_ref[plan_ref[0, 32 + p]]).astype(out_ref.dtype)


def delta_kernel(grad_ref, out_ref, delta_ref):
    ones = jnp.ones((8, width), jnp.bfloat16)
    for h in range(kv_heads):
        cut = slice(h * group, (h + 1) * group)
        grad = grad_ref[...].astype(jnp.float32)[:, cut].reshape(columns, width)
        out = out_ref[...].astype(jnp.float32)[:, cut].reshape(columns, width)
        product = grad * out
        high = product.astype(jnp.bfloat16)
        rest = (product - high.astype(jnp.float32)).astype(jnp.bfloat16)
        delta_ref[h : h + 1] = (nt(ones, high) + nt(ones, rest))[0:1]


def attention_kernel(*refs):
    info_ref = refs[0]
    message_refs = refs[1 : 1 + share]
    delta_refs = refs[1 + share : 1 + 2 * share]
    window_ref = refs[1 + 2 * share]
    results = refs[2 + 2 * share :]
    result_refs = results[:share]
    own_grad_ref, window_grad_ref, bias_ref, key_acc_ref, value_acc_ref = results[share:]
    place = info_ref[share : share + 1, :width]
    row = lax.broadcasted_iota(jnp.int32, (window, width), 0)
    stretch = lax.shift_right_logical(row, 6)
    source = lax.div(row, piece) & 7
    inside = lax.div(row, 8 * piece) * piece + (row & (piece - 1))
    key_at = source * chunk + inside
    key_at = jnp.where(
        lax.div(source, share) >= lax.div(place, share), key_at, key_at + span
    )
    for b in range(share):
        key_at = jnp.where(
            stretch == 8 + b, row - b * chunk + (place ^ b) * chunk, key_at
        )

    def own_rows(b, h, kind):
        start = local_kv * 2 * columns + (h * 2 + kind) * chunk
        return message_refs[b][start : start + chunk]

    for b in range(share):
        for c in range(0, columns, width):
            token = lax.shift_right_logical(
                c + lax.broadcasted_iota(jnp.int32, (1, width), 1), 3
            )
            last = span + (place ^ b) * chunk + token
            allowed = (key_at <= last) & (key_at >= info_ref[b : b + 1, c : c + width])
            bias_ref[:, b * columns + c : b * columns + c + width] = jnp.where(
                allowed, 0.0, masked
            )
    for h in range(local_kv):
        key = jnp.concatenate(
            [window_ref[h, 0]] + [own_rows(k, h, 0) for k in range(share)], axis=0
        )
        value = jnp.concatenate(
            [window_ref[h, 1]] + [own_rows(k, h, 1) for k in range(share)], axis=0
        )
        for b in range(0, share, merged):
            several = range(b, b + merged)
            query = jnp.concatenate(
                [message_refs[k][h * columns : (h + 1) * columns] for k in several], axis=0
            )
            start = (local_kv + h) * columns
            grad = jnp.concatenate(
                [message_refs[k][start : start + columns] for k in several], axis=0
            )
            delta = jnp.concatenate([delta_refs[k][h : h + 1] for k in several], axis=1)
            bias = bias_ref[:, b * columns : (b + merged) * columns]
            scores = nt(key, query) * (factor * log2e) + bias
            top = jnp.max(scores, axis=0, keepdims=True)
            exps = jnp.exp2(scores - top)
            total = jnp.sum(exps, axis=0, keepdims=True)
            probs = exps * (1.0 / total)
            grad_scores = (probs * (nt(value, grad) - delta)).astype(low)
            value_part = jnp.dot(
                probs.astype(low), grad, preferred_element_type=jnp.float32
            )
            key_part = jnp.dot(grad_scores, query, preferred_element_type=jnp.float32)
            query_part = lax.dot_general(
                key, grad_scores, (((0,), (0,)), ((), ())), preferred_element_type=jnp.float32
            )
            query_part = (jnp.transpose(query_part) * factor).astype(low)
            for k in several:
                result_refs[k][h * columns : (h + 1) * columns] = query_part[
                    (k - b) * columns : (k - b + 1) * columns
                ]
            if b > 0:
                key_part = key_part + key_acc_ref[h]
                value_part = value_part + value_acc_ref[h]
            if b + merged < share:
                key_acc_ref[h] = key_part
                value_acc_ref[h] = value_part
            else:
                key_part = key_part * factor
                window_grad_ref[h, 0] = key_part[:span].astype(low)
                window_grad_ref[h, 1] = value_part[:span].astype(low)
                for k in range(share):
                    at = slice(span + k * chunk, span + (k + 1) * chunk)
                    for kind, part in enumerate((key_part, value_part)):
                        start = (h * 2 + kind) * chunk
                        if k == 0:
                            own_grad_ref[start : start + chunk] = part[at]
                        else:
                            start = start + local_kv * columns
                            result_refs[k][start : start + chunk] = part[at].astype(low)


vmem = pl.BlockSpec(memory_space=pltpu.VMEM)


def grant(mib):
    return pltpu.CompilerParams(vmem_limit_bytes=mib * 2**20)


def near(array):
    return pltpu.with_memory_space_constraint(array, pltpu.VMEM)


smem = pl.BlockSpec(memory_space=pltpu.SMEM)
low = jnp.bfloat16


def trade(array, b):
    return lax.ppermute(array, "z", [(i, i ^ b) for i in range(8)])


def route(array, axes):
    return lax.all_to_all(array, axes, split_axis=0, concat_axis=0, tiled=True)


def plan(span_order, z):
    spans = jnp.transpose(span_order).reshape(32)
    kind = lax.broadcasted_iota(jnp.int32, (4, 32, 32), 0)
    other = lax.broadcasted_iota(jnp.int32, (4, 32, 32), 2)
    wanted = spans[None, :, None] + jnp.where(kind == 0, -1, 1)
    found = jnp.where(kind == 0, other, other - 32)
    found = jnp.sum(jnp.where(spans[None, None, :] == wanted, found, 0), axis=2)
    kind = lax.broadcasted_iota(jnp.int32, (4, 32), 0)
    found = jnp.where(kind == 2, z, found + jnp.where(kind == 1, 32, 0))
    return near(found.reshape(1, 128))


def bounds(span_order, doc_lengths, query_index, half, z):
    base = (span_order[query_index, half] - 1) * span
    ends = jnp.cumsum(doc_lengths)
    block = lax.broadcasted_iota(jnp.int32, (share, chunk, 64), 0)
    token = lax.broadcasted_iota(jnp.int32, (share, chunk, 64), 1)
    at = base + span + (z ^ block) * chunk + token
    lows = jnp.max(jnp.where(ends[None, None, :] <= at, ends[None, None, :], 0), axis=2) - base
    lows = jnp.broadcast_to(lows[:, :, None], (share, chunk, group)).reshape(share, columns)
    places = jnp.broadcast_to(z, (1, columns)).astype(jnp.int32)
    return near(jnp.concatenate([lows, places], axis=0))


def shards(queries, keys, values, attention_out, out_grad, span_order, doc_lengths):
    z = lax.axis_index("z")
    mine = lax.rem(z, share)
    query_index = (lax.axis_index("yh") * 4 + lax.axis_index("x")) * 2 + lax.axis_index("c")
    table = plan(span_order, z)
    own = jnp.stack([jnp.transpose(keys, (1, 0, 2)), jnp.transpose(values, (1, 0, 2))], axis=1)
    own = own.reshape(share, 32, piece, width)
    pieces = route(jnp.transpose(own, (1, 0, 2, 3)), plane_axes)
    delta = pl.pallas_call(
        delta_kernel,
        compiler_params=grant(8),
        out_shape=jax.ShapeDtypeStruct((kv_heads, columns), jnp.float32),
        in_specs=[vmem, vmem],
        out_specs=vmem,
    )(out_grad, attention_out).reshape(share, local_kv, columns)

    def per_share(array):
        array = array.reshape(chunk, share, local_kv, group, width)
        return jnp.transpose(array, (1, 2, 0, 3, 4)).reshape(share, local_kv * columns, width)

    whole = jnp.concatenate(
        [per_share(queries), per_share(out_grad), own.reshape(share, -1, width)], axis=1
    )
    messages = []
    deltas = []
    for b in range(share):
        message = lax.dynamic_index_in_dim(whole, mine ^ b, 0, keepdims=False)
        part = lax.dynamic_index_in_dim(delta, mine ^ b, 0, keepdims=False)
        messages.append(trade(message, b) if b else message)
        deltas.append(trade(part, b) if b else part)

    spread = pl.pallas_call(
        expand_kernel,
        compiler_params=grant(8),
        out_shape=pltpu.VMEM((32, 8, piece, width), low),
        in_specs=[vmem, vmem],
        out_specs=vmem,
        scratch_shapes=[
            pltpu.SMEM((1, 128), jnp.int32),
            pltpu.VMEM((32, share, piece, width), low),
        ],
    )(table, near(pieces))
    around = route(spread.reshape(256, piece, width), all_axes)
    back_rows = local_kv * (columns + 2 * chunk)
    results = pl.pallas_call(
        attention_kernel,
        compiler_params=grant(32),
        out_shape=tuple(
            [pltpu.VMEM((local_kv * columns, width), low)]
            + [pltpu.VMEM((back_rows, width), low)] * (share - 1)
            + [pltpu.VMEM((local_kv * 2 * chunk, width), jnp.float32)]
            + [pltpu.VMEM((local_kv, 2, span, width), low)]
        ),
        in_specs=[vmem] * (2 * share + 2),
        out_specs=tuple([vmem] * (share + 2)),
        scratch_shapes=[
            pltpu.VMEM((window, share * columns), jnp.float32),
            pltpu.VMEM((local_kv, window, width), jnp.float32),
            pltpu.VMEM((local_kv, window, width), jnp.float32),
        ],
    )(
        bounds(span_order, doc_lengths, query_index, lax.axis_index("yl"), z),
        *[near(m) for m in messages],
        *[near(d) for d in deltas],
        near(around.reshape(local_kv, 2, span, width)),
    )
    parts = route(results[-1].reshape(256, piece, width), all_axes)
    query_grads = [results[0]]
    own_grads = [results[share]]
    for b in range(1, share):
        got = trade(results[b], b)
        query_grads.append(got[: local_kv * columns])
        own_grads.append(got[local_kv * columns :])
    sums = pl.pallas_call(
        reduce_kernel,
        compiler_params=grant(8),
        out_shape=pltpu.VMEM((32, share, piece, width), low),
        in_specs=[vmem, vmem],
        out_specs=vmem,
        scratch_shapes=[
            pltpu.SMEM((1, 128), jnp.int32),
            pltpu.VMEM((32, share, piece, width), jnp.float32),
            pltpu.VMEM((33, share, piece, width), jnp.float32),
        ],
    )(table, near(parts.reshape(32, 8, piece, width)))
    back = route(sums, plane_axes)

    def arranged(members):
        found = []
        for e in range(share):
            chosen = members[0]
            for b in range(1, share):
                chosen = jnp.where((mine ^ b) == e, members[b], chosen)
            found.append(chosen)
        return jnp.stack(found)

    query_grad = arranged(query_grads).reshape(share, local_kv, chunk, group, width)
    query_grad = jnp.transpose(query_grad, (2, 0, 1, 3, 4)).reshape(chunk, heads, width)
    local = arranged([m.astype(jnp.float32) for m in own_grads])
    back, query_grad, local = lax.optimization_barrier((back, query_grad, local))
    back = jnp.transpose(back, (1, 0, 2, 3)).reshape(share, -1, width)
    both = (local + back).reshape(kv_heads, 2, chunk, width)
    both = jnp.transpose(both, (1, 2, 0, 3)).astype(low)
    return query_grad, both[0], both[1]


def solution(mesh):
    fine = Mesh(mesh.devices.reshape(2, 8, 2, 4, 2), ("yl", "z", "yh", "x", "c"))
    rows = P(row_axes, None, None)
    return jax.shard_map(
        shards,
        mesh=fine,
        in_specs=(rows, rows, rows, rows, rows, P(), P()),
        out_specs=(rows, rows, rows),
        check_vma=False,
    )
```

```python
import jax
import jax.numpy as jnp
from jax import lax
from jax.experimental import pallas as pl
from jax.experimental.pallas import tpu as pltpu
from jax.sharding import Mesh, PartitionSpec as P


span = 512
chunk = 64
group = 8
width = 128
kv_heads = 4
heads = 32
share = 2
local_kv = kv_heads // share
piece = 16 // share
window = span + share * chunk
columns = chunk * group
merged = 2
row_axes = ("yh", "x", "c", "yl", "z")
plane_axes = ("yl", "yh", "x", "c")
all_axes = ("yl", "yh", "x", "c", "z")
masked = -1e30
log2e = 1.4426950408889634
factor = width ** -0.5


def nt(a, b):
    return lax.dot_general(
        a, b, (((1,), (1,)), ((), ())), preferred_element_type=jnp.float32
    )


def expand_kernel(table_ref, pieces_ref, out_ref, plan_ref, prev_ref, sem):
    fetch = pltpu.make_async_copy(table_ref, plan_ref, sem)
    fetch.start()
    for j in range(share, 8):
        out_ref[:, j] = pieces_ref[:, j % share]
    fetch.wait()
    z = plan_ref[0, 64]
    for p in range(32):
        prev_ref[p] = pieces_ref[plan_ref[0, p]]
    for j in range(share):
        out_ref[:, j] = prev_ref[:, j]
    for j in range(share, 8, share):
        @pl.when(j // share <= lax.div(z, share))
        def _():
            for e in range(share):
                out_ref[:, j + e] = prev_ref[:, e]


def reduce_kernel(table_ref, parts_ref, out_ref, plan_ref, own_ref, prev_ref, sem):
    fetch = pltpu.make_async_copy(table_ref, plan_ref, sem)
    fetch.start()
    z = jnp.max(jnp.broadcast_to(table_ref[0:1, 64:65], (piece, width)), axis=0, keepdims=True)
    mask = [
        jnp.broadcast_to(j // share > lax.div(z, share), (piece, width))[None]
        for j in range(8)
    ]
    prev_ref[32] = jnp.zeros((share, piece, width), jnp.float32)
    for e in range(share):
        own = jnp.zeros((32, piece, width), jnp.float32)
        prev = jnp.zeros((32, piece, width), jnp.float32)
        for j in range(e, 8, share):
            part = parts_ref[:, j].astype(jnp.float32)
            own = own + jnp.where(mask[j], part, 0.0)
            prev = prev + jnp.where(mask[j], 0.0, part)
        own_ref[:, e] = own
        prev_ref[:32, e] = prev
    fetch.wait()
    for p in range(32):
        out_ref[p] = (own_ref[p] + prev_ref[plan_ref[0, 32 + p]]).astype(out_ref.dtype)


def delta_kernel(grad_ref, out_ref, delta_ref):
    ones = jnp.ones((8, width), jnp.bfloat16)
    for h in range(kv_heads):
        cut = slice(h * group, (h + 1) * group)
        grad = grad_ref[...].astype(jnp.float32)[:, cut].reshape(columns, width)
        out = out_ref[...].astype(jnp.float32)[:, cut].reshape(columns, width)
        product = grad * out
        high = product.astype(jnp.bfloat16)
        rest = (product - high.astype(jnp.float32)).astype(jnp.bfloat16)
        delta_ref[h : h + 1] = (nt(ones, high) + nt(ones, rest))[0:1]


def attention_kernel(*refs):
    info_ref = refs[0]
    message_refs = refs[1 : 1 + share]
    delta_refs = refs[1 + share : 1 + 2 * share]
    window_ref = refs[1 + 2 * share]
    results = refs[2 + 2 * share :]
    result_refs = results[:share]
    own_grad_ref, window_grad_ref, bias_ref, key_acc_ref, value_acc_ref = results[share:]
    place = info_ref[share : share + 1, :width]
    row = lax.broadcasted_iota(jnp.int32, (window, width), 0)
    stretch = lax.shift_right_logical(row, 6)
    source = lax.div(row, piece) & 7
    inside = lax.div(row, 8 * piece) * piece + (row & (piece - 1))
    key_at = source * chunk + inside
    key_at = jnp.where(
        lax.div(source, share) >= lax.div(place, share), key_at, key_at + span
    )
    for b in range(share):
        key_at = jnp.where(
            stretch == 8 + b, row - b * chunk + (place ^ b) * chunk, key_at
        )

    def own_rows(b, h, kind):
        start = local_kv * 2 * columns + (h * 2 + kind) * chunk
        return message_refs[b][start : start + chunk]

    for b in range(share):
        for c in range(0, columns, width):
            token = lax.shift_right_logical(
                c + lax.broadcasted_iota(jnp.int32, (1, width), 1), 3
            )
            last = span + (place ^ b) * chunk + token
            allowed = (key_at <= last) & (key_at >= info_ref[b : b + 1, c : c + width])
            bias_ref[:, b * columns + c : b * columns + c + width] = jnp.where(
                allowed, 0.0, masked
            )
    for h in range(local_kv):
        key = jnp.concatenate(
            [window_ref[h, 0]] + [own_rows(k, h, 0) for k in range(share)], axis=0
        )
        value = jnp.concatenate(
            [window_ref[h, 1]] + [own_rows(k, h, 1) for k in range(share)], axis=0
        )
        for b in range(0, share, merged):
            several = range(b, b + merged)
            query = jnp.concatenate(
                [message_refs[k][h * columns : (h + 1) * columns] for k in several], axis=0
            )
            start = (local_kv + h) * columns
            grad = jnp.concatenate(
                [message_refs[k][start : start + columns] for k in several], axis=0
            )
            delta = jnp.concatenate([delta_refs[k][h : h + 1] for k in several], axis=1)
            bias = bias_ref[:, b * columns : (b + merged) * columns]
            scores = nt(key, query) * (factor * log2e) + bias
            top = jnp.max(scores, axis=0, keepdims=True)
            exps = jnp.exp2(scores - top)
            total = jnp.sum(exps, axis=0, keepdims=True)
            probs = exps * (1.0 / total)
            grad_scores = (probs * (nt(value, grad) - delta)).astype(low)
            value_part = jnp.dot(
                probs.astype(low), grad, preferred_element_type=jnp.float32
            )
            key_part = jnp.dot(grad_scores, query, preferred_element_type=jnp.float32)
            query_part = lax.dot_general(
                key, grad_scores, (((0,), (0,)), ((), ())), preferred_element_type=jnp.float32
            )
            query_part = (jnp.transpose(query_part) * factor).astype(low)
            for k in several:
                result_refs[k][h * columns : (h + 1) * columns] = query_part[
                    (k - b) * columns : (k - b + 1) * columns
                ]
            if b > 0:
                key_part = key_part + key_acc_ref[h]
                value_part = value_part + value_acc_ref[h]
            if b + merged < share:
                key_acc_ref[h] = key_part
                value_acc_ref[h] = value_part
            else:
                key_part = key_part * factor
                window_grad_ref[h, 0] = key_part[:span].astype(low)
                window_grad_ref[h, 1] = value_part[:span].astype(low)
                for k in range(share):
                    at = slice(span + k * chunk, span + (k + 1) * chunk)
                    for kind, part in enumerate((key_part, value_part)):
                        start = (h * 2 + kind) * chunk
                        if k == 0:
                            own_grad_ref[start : start + chunk] = part[at]
                        else:
                            start = start + local_kv * columns
                            result_refs[k][start : start + chunk] = part[at].astype(low)


vmem = pl.BlockSpec(memory_space=pltpu.VMEM)


def grant(mib):
    return pltpu.CompilerParams(vmem_limit_bytes=mib * 2**20)


def near(array):
    return pltpu.with_memory_space_constraint(array, pltpu.VMEM)


smem = pl.BlockSpec(memory_space=pltpu.SMEM)
low = jnp.bfloat16


def trade(array, b):
    return lax.ppermute(array, "z", [(i, i ^ b) for i in range(8)])


def route(array, axes):
    return lax.all_to_all(array, axes, split_axis=0, concat_axis=0, tiled=True)


def plan(span_order, z):
    spans = jnp.transpose(span_order).reshape(32)
    kind = lax.broadcasted_iota(jnp.int32, (4, 32, 32), 0)
    other = lax.broadcasted_iota(jnp.int32, (4, 32, 32), 2)
    wanted = spans[None, :, None] + jnp.where(kind == 0, -1, 1)
    found = jnp.where(kind == 0, other, other - 32)
    found = jnp.sum(jnp.where(spans[None, None, :] == wanted, found, 0), axis=2)
    kind = lax.broadcasted_iota(jnp.int32, (4, 32), 0)
    found = jnp.where(kind == 2, z, found + jnp.where(kind == 1, 32, 0))
    return near(found.reshape(1, 128))


def bounds(span_order, doc_lengths, query_index, half, z):
    base = (span_order[query_index, half] - 1) * span
    ends = jnp.cumsum(doc_lengths)
    block = lax.broadcasted_iota(jnp.int32, (share, chunk, 64), 0)
    token = lax.broadcasted_iota(jnp.int32, (share, chunk, 64), 1)
    at = base + span + (z ^ block) * chunk + token
    lows = jnp.max(jnp.where(ends[None, None, :] <= at, ends[None, None, :], 0), axis=2) - base
    lows = jnp.broadcast_to(lows[:, :, None], (share, chunk, group)).reshape(share, columns)
    places = jnp.broadcast_to(z, (1, columns)).astype(jnp.int32)
    return near(jnp.concatenate([lows, places], axis=0))


def shards(queries, keys, values, attention_out, out_grad, span_order, doc_lengths):
    z = lax.axis_index("z")
    mine = lax.rem(z, share)
    query_index = (lax.axis_index("yh") * 4 + lax.axis_index("x")) * 2 + lax.axis_index("c")
    table = plan(span_order, z)
    own = jnp.stack([jnp.transpose(keys, (1, 0, 2)), jnp.transpose(values, (1, 0, 2))], axis=1)
    own = own.reshape(share, 32, piece, width)
    pieces = route(jnp.transpose(own, (1, 0, 2, 3)), plane_axes)
    delta = pl.pallas_call(
        delta_kernel,
        compiler_params=grant(8),
        out_shape=jax.ShapeDtypeStruct((kv_heads, columns), jnp.float32),
        in_specs=[vmem, vmem],
        out_specs=vmem,
    )(out_grad, attention_out).reshape(share, local_kv, columns)

    def per_share(array):
        array = array.reshape(chunk, share, local_kv, group, width)
        return jnp.transpose(array, (1, 2, 0, 3, 4)).reshape(share, local_kv * columns, width)

    whole = jnp.concatenate(
        [per_share(queries), per_share(out_grad), own.reshape(share, -1, width)], axis=1
    )
    messages = []
    deltas = []
    for b in range(share):
        message = lax.dynamic_index_in_dim(whole, mine ^ b, 0, keepdims=False)
        part = lax.dynamic_index_in_dim(delta, mine ^ b, 0, keepdims=False)
        messages.append(trade(message, b) if b else message)
        deltas.append(trade(part, b) if b else part)

    spread = pl.pallas_call(
        expand_kernel,
        compiler_params=grant(8),
        out_shape=pltpu.VMEM((32, 8, piece, width), low),
        in_specs=[vmem, vmem],
        out_specs=vmem,
        scratch_shapes=[
            pltpu.SMEM((1, 128), jnp.int32),
            pltpu.VMEM((32, share, piece, width), low),
            pltpu.SemaphoreType.DMA(()),
        ],
    )(table, near(pieces))
    around = route(spread.reshape(256, piece, width), all_axes)
    back_rows = local_kv * (columns + 2 * chunk)
    results = pl.pallas_call(
        attention_kernel,
        compiler_params=grant(32),
        out_shape=tuple(
            [pltpu.VMEM((local_kv * columns, width), low)]
            + [pltpu.VMEM((back_rows, width), low)] * (share - 1)
            + [pltpu.VMEM((local_kv * 2 * chunk, width), jnp.float32)]
            + [pltpu.VMEM((local_kv, 2, span, width), low)]
        ),
        in_specs=[vmem] * (2 * share + 2),
        out_specs=tuple([vmem] * (share + 2)),
        scratch_shapes=[
            pltpu.VMEM((window, share * columns), jnp.float32),
            pltpu.VMEM((local_kv, window, width), jnp.float32),
            pltpu.VMEM((local_kv, window, width), jnp.float32),
        ],
    )(
        bounds(span_order, doc_lengths, query_index, lax.axis_index("yl"), z),
        *[near(m) for m in messages],
        *[near(d) for d in deltas],
        near(around.reshape(local_kv, 2, span, width)),
    )
    parts = route(results[-1].reshape(256, piece, width), all_axes)
    query_grads = [results[0]]
    own_grads = [results[share]]
    for b in range(1, share):
        got = trade(results[b], b)
        query_grads.append(got[: local_kv * columns])
        own_grads.append(got[local_kv * columns :])
    sums = pl.pallas_call(
        reduce_kernel,
        compiler_params=grant(8),
        out_shape=pltpu.VMEM((32, share, piece, width), low),
        in_specs=[vmem, vmem],
        out_specs=vmem,
        scratch_shapes=[
            pltpu.SMEM((1, 128), jnp.int32),
            pltpu.VMEM((32, share, piece, width), jnp.float32),
            pltpu.VMEM((33, share, piece, width), jnp.float32),
            pltpu.SemaphoreType.DMA(()),
        ],
    )(table, near(parts.reshape(32, 8, piece, width)))
    back = route(sums, plane_axes)

    def arranged(members):
        found = []
        for e in range(share):
            chosen = members[0]
            for b in range(1, share):
                chosen = jnp.where((mine ^ b) == e, members[b], chosen)
            found.append(chosen)
        return jnp.stack(found)

    query_grad = arranged(query_grads).reshape(share, local_kv, chunk, group, width)
    query_grad = jnp.transpose(query_grad, (2, 0, 1, 3, 4)).reshape(chunk, heads, width)
    local = arranged([m.astype(jnp.float32) for m in own_grads])
    back, query_grad, local = lax.optimization_barrier((back, query_grad, local))
    back = jnp.transpose(back, (1, 0, 2, 3)).reshape(share, -1, width)
    both = (local + back).reshape(kv_heads, 2, chunk, width)
    both = jnp.transpose(both, (1, 2, 0, 3)).astype(low)
    return query_grad, both[0], both[1]


def solution(mesh):
    fine = Mesh(mesh.devices.reshape(2, 8, 2, 4, 2), ("yl", "z", "yh", "x", "c"))
    rows = P(row_axes, None, None)
    return jax.shard_map(
        shards,
        mesh=fine,
        in_specs=(rows, rows, rows, rows, rows, P(), P()),
        out_specs=(rows, rows, rows),
        check_vma=False,
    )
```

```python
import jax
import jax.numpy as jnp
from jax import lax
from jax.experimental import pallas as pl
from jax.experimental.pallas import tpu as pltpu
from jax.sharding import Mesh, PartitionSpec as P


span = 512
chunk = 64
group = 8
width = 128
kv_heads = 4
heads = 32
share = 2
local_kv = kv_heads // share
piece = 16 // share
window = span + share * chunk
columns = chunk * group
merged = 2
row_axes = ("yh", "x", "c", "yl", "z")
plane_axes = ("yl", "yh", "x", "c")
all_axes = ("yl", "yh", "x", "c", "z")
masked = -1e30
log2e = 1.4426950408889634
factor = width ** -0.5


def nt(a, b):
    return lax.dot_general(
        a, b, (((1,), (1,)), ((), ())), preferred_element_type=jnp.float32
    )


def expand_kernel(table_ref, pieces_ref, out_ref, plan_ref, prev_ref, sem):
    fetch = pltpu.make_async_copy(table_ref, plan_ref, sem)
    fetch.start()
    for j in range(share, 8):
        out_ref[:, j] = pieces_ref[:, j % share]
    fetch.wait()
    z = plan_ref[0, 64]
    for p in range(32):
        prev_ref[p] = pieces_ref[plan_ref[0, p]]
    for j in range(share):
        out_ref[:, j] = prev_ref[:, j]
    for j in range(share, 8, share):
        @pl.when(j // share <= lax.div(z, share))
        def _():
            for e in range(share):
                out_ref[:, j + e] = prev_ref[:, e]


def reduce_kernel(table_ref, parts_ref, out_ref, plan_ref, own_ref, prev_ref, sem):
    fetch = pltpu.make_async_copy(table_ref, plan_ref, sem)
    fetch.start()
    z = jnp.max(jnp.broadcast_to(table_ref[0:1, 64:65], (piece, width)), axis=0, keepdims=True)
    mask = [
        jnp.broadcast_to(j // share > lax.div(z, share), (piece, width))[None]
        for j in range(8)
    ]
    prev_ref[32] = jnp.zeros((share, piece, width), jnp.float32)
    for e in range(share):
        own = jnp.zeros((32, piece, width), jnp.float32)
        prev = jnp.zeros((32, piece, width), jnp.float32)
        for j in range(e, 8, share):
            part = parts_ref[:, j].astype(jnp.float32)
            own = own + jnp.where(mask[j], part, 0.0)
            prev = prev + jnp.where(mask[j], 0.0, part)
        own_ref[:, e] = own
        prev_ref[:32, e] = prev
    fetch.wait()
    for p in range(32):
        out_ref[p] = (own_ref[p] + prev_ref[plan_ref[0, 32 + p]]).astype(out_ref.dtype)


def delta_kernel(grad_ref, out_ref, delta_ref):
    ones = jnp.ones((8, width), jnp.bfloat16)
    for h in range(kv_heads):
        cut = slice(h * group, (h + 1) * group)
        grad = grad_ref[...].astype(jnp.float32)[:, cut].reshape(columns, width)
        out = out_ref[...].astype(jnp.float32)[:, cut].reshape(columns, width)
        product = grad * out
        high = product.astype(jnp.bfloat16)
        rest = (product - high.astype(jnp.float32)).astype(jnp.bfloat16)
        delta_ref[h : h + 1] = (nt(ones, high) + nt(ones, rest))[0:1]


def attention_kernel(*refs):
    info_ref = refs[0]
    message_refs = refs[1 : 1 + share]
    delta_refs = refs[1 + share : 1 + 2 * share]
    window_ref = refs[1 + 2 * share]
    results = refs[2 + 2 * share :]
    result_refs = results[:share]
    own_grad_ref, window_grad_ref, bias_ref, key_acc_ref, value_acc_ref = results[share:]
    place = info_ref[share : share + 1, :width]
    row = lax.broadcasted_iota(jnp.int32, (window, width), 0)
    stretch = lax.shift_right_logical(row, 6)
    shift = piece.bit_length() - 1
    source = lax.shift_right_logical(row, shift) & 7
    inside = lax.shift_right_logical(row, shift + 3) * piece + (row & (piece - 1))
    key_at = source * chunk + inside
    key_at = jnp.where(
        (source | (share - 1)) >= place, key_at, key_at + span
    )
    for b in range(share):
        key_at = jnp.where(
            stretch == 8 + b, row - b * chunk + (place ^ b) * chunk, key_at
        )

    def own_rows(b, h, kind):
        start = local_kv * 2 * columns + (h * 2 + kind) * chunk
        return message_refs[b][start : start + chunk]

    for b in range(share):
        for c in range(0, columns, width):
            token = lax.shift_right_logical(
                c + lax.broadcasted_iota(jnp.int32, (1, width), 1), 3
            )
            last = span + (place ^ b) * chunk + token
            first = info_ref[b : b + 1, c : c + width]
            allowed = (key_at - first).astype(jnp.uint32) <= (last - first).astype(jnp.uint32)
            bias_ref[:, b * columns + c : b * columns + c + width] = jnp.where(
                allowed, 0.0, masked
            )
    for h in range(local_kv):
        key = jnp.concatenate(
            [window_ref[h, 0]] + [own_rows(k, h, 0) for k in range(share)], axis=0
        )
        value = jnp.concatenate(
            [window_ref[h, 1]] + [own_rows(k, h, 1) for k in range(share)], axis=0
        )
        for b in range(0, share, merged):
            several = range(b, b + merged)
            query = jnp.concatenate(
                [message_refs[k][h * columns : (h + 1) * columns] for k in several], axis=0
            )
            start = (local_kv + h) * columns
            grad = jnp.concatenate(
                [message_refs[k][start : start + columns] for k in several], axis=0
            )
            delta = jnp.concatenate([delta_refs[k][h : h + 1] for k in several], axis=1)
            bias = bias_ref[:, b * columns : (b + merged) * columns]
            scores = nt(key, query) * (factor * log2e) + bias
            top = jnp.max(scores, axis=0, keepdims=True)
            exps = jnp.exp2(scores - top)
            total = jnp.sum(exps, axis=0, keepdims=True)
            probs = exps * (1.0 / total)
            grad_scores = (probs * (nt(value, grad) - delta)).astype(low)
            value_part = jnp.dot(
                probs.astype(low), grad, preferred_element_type=jnp.float32
            )
            key_part = jnp.dot(grad_scores, query, preferred_element_type=jnp.float32)
            query_part = lax.dot_general(
                key, grad_scores, (((0,), (0,)), ((), ())), preferred_element_type=jnp.float32
            )
            query_part = (jnp.transpose(query_part) * factor).astype(low)
            for k in several:
                result_refs[k][h * columns : (h + 1) * columns] = query_part[
                    (k - b) * columns : (k - b + 1) * columns
                ]
            if b > 0:
                key_part = key_part + key_acc_ref[h]
                value_part = value_part + value_acc_ref[h]
            if b + merged < share:
                key_acc_ref[h] = key_part
                value_acc_ref[h] = value_part
            else:
                key_part = key_part * factor
                window_grad_ref[h, 0] = key_part[:span].astype(low)
                window_grad_ref[h, 1] = value_part[:span].astype(low)
                for k in range(share):
                    at = slice(span + k * chunk, span + (k + 1) * chunk)
                    for kind, part in enumerate((key_part, value_part)):
                        start = (h * 2 + kind) * chunk
                        if k == 0:
                            own_grad_ref[start : start + chunk] = part[at]
                        else:
                            start = start + local_kv * columns
                            result_refs[k][start : start + chunk] = part[at].astype(low)


vmem = pl.BlockSpec(memory_space=pltpu.VMEM)


def grant(mib):
    return pltpu.CompilerParams(vmem_limit_bytes=mib * 2**20)


def near(array):
    return pltpu.with_memory_space_constraint(array, pltpu.VMEM)


smem = pl.BlockSpec(memory_space=pltpu.SMEM)
low = jnp.bfloat16


def trade(array, b):
    return lax.ppermute(array, "z", [(i, i ^ b) for i in range(8)])


def route(array, axes):
    return lax.all_to_all(array, axes, split_axis=0, concat_axis=0, tiled=True)


def plan(span_order, z):
    spans = jnp.transpose(span_order).reshape(32)
    kind = lax.broadcasted_iota(jnp.int32, (4, 32, 32), 0)
    other = lax.broadcasted_iota(jnp.int32, (4, 32, 32), 2)
    wanted = spans[None, :, None] + jnp.where(kind == 0, -1, 1)
    found = jnp.where(kind == 0, other, other - 32)
    found = jnp.sum(jnp.where(spans[None, None, :] == wanted, found, 0), axis=2)
    kind = lax.broadcasted_iota(jnp.int32, (4, 32), 0)
    found = jnp.where(kind == 2, z, found + jnp.where(kind == 1, 32, 0))
    return near(found.reshape(1, 128))


def bounds(span_order, doc_lengths, query_index, half, z):
    base = (span_order[query_index, half] - 1) * span
    ends = jnp.cumsum(doc_lengths)
    block = lax.broadcasted_iota(jnp.int32, (share, chunk, 64), 0)
    token = lax.broadcasted_iota(jnp.int32, (share, chunk, 64), 1)
    at = base + span + (z ^ block) * chunk + token
    lows = jnp.max(jnp.where(ends[None, None, :] <= at, ends[None, None, :], 0), axis=2) - base
    lows = jnp.broadcast_to(lows[:, :, None], (share, chunk, group)).reshape(share, columns)
    places = jnp.broadcast_to(z, (1, columns)).astype(jnp.int32)
    return near(jnp.concatenate([lows, places], axis=0))


def shards(queries, keys, values, attention_out, out_grad, span_order, doc_lengths):
    z = lax.axis_index("z")
    mine = lax.rem(z, share)
    query_index = (lax.axis_index("yh") * 4 + lax.axis_index("x")) * 2 + lax.axis_index("c")
    table = plan(span_order, z)
    own = jnp.stack([jnp.transpose(keys, (1, 0, 2)), jnp.transpose(values, (1, 0, 2))], axis=1)
    own = own.reshape(share, 32, piece, width)
    pieces = route(jnp.transpose(own, (1, 0, 2, 3)), plane_axes)
    delta = pl.pallas_call(
        delta_kernel,
        compiler_params=grant(8),
        out_shape=jax.ShapeDtypeStruct((kv_heads, columns), jnp.float32),
        in_specs=[vmem, vmem],
        out_specs=vmem,
    )(out_grad, attention_out).reshape(share, local_kv, columns)

    def per_share(array):
        array = array.reshape(chunk, share, local_kv, group, width)
        return jnp.transpose(array, (1, 2, 0, 3, 4)).reshape(share, local_kv * columns, width)

    whole = jnp.concatenate(
        [per_share(queries), per_share(out_grad), own.reshape(share, -1, width)], axis=1
    )
    messages = []
    deltas = []
    for b in range(share):
        message = lax.dynamic_index_in_dim(whole, mine ^ b, 0, keepdims=False)
        part = lax.dynamic_index_in_dim(delta, mine ^ b, 0, keepdims=False)
        messages.append(trade(message, b) if b else message)
        deltas.append(trade(part, b) if b else part)

    spread = pl.pallas_call(
        expand_kernel,
        compiler_params=grant(8),
        out_shape=pltpu.VMEM((32, 8, piece, width), low),
        in_specs=[vmem, vmem],
        out_specs=vmem,
        scratch_shapes=[
            pltpu.SMEM((1, 128), jnp.int32),
            pltpu.VMEM((32, share, piece, width), low),
            pltpu.SemaphoreType.DMA(()),
        ],
    )(table, near(pieces))
    around = route(spread.reshape(256, piece, width), all_axes)
    back_rows = local_kv * (columns + 2 * chunk)
    results = pl.pallas_call(
        attention_kernel,
        compiler_params=grant(32),
        out_shape=tuple(
            [pltpu.VMEM((local_kv * columns, width), low)]
            + [pltpu.VMEM((back_rows, width), low)] * (share - 1)
            + [pltpu.VMEM((local_kv * 2 * chunk, width), jnp.float32)]
            + [pltpu.VMEM((local_kv, 2, span, width), low)]
        ),
        in_specs=[vmem] * (2 * share + 2),
        out_specs=tuple([vmem] * (share + 2)),
        scratch_shapes=[
            pltpu.VMEM((window, share * columns), jnp.float32),
            pltpu.VMEM((local_kv, window, width), jnp.float32),
            pltpu.VMEM((local_kv, window, width), jnp.float32),
        ],
    )(
        bounds(span_order, doc_lengths, query_index, lax.axis_index("yl"), z),
        *[near(m) for m in messages],
        *[near(d) for d in deltas],
        near(around.reshape(local_kv, 2, span, width)),
    )
    parts = route(results[-1].reshape(256, piece, width), all_axes)
    query_grads = [results[0]]
    own_grads = [results[share]]
    for b in range(1, share):
        got = trade(results[b], b)
        query_grads.append(got[: local_kv * columns])
        own_grads.append(got[local_kv * columns :])
    sums = pl.pallas_call(
        reduce_kernel,
        compiler_params=grant(8),
        out_shape=pltpu.VMEM((32, share, piece, width), low),
        in_specs=[vmem, vmem],
        out_specs=vmem,
        scratch_shapes=[
            pltpu.SMEM((1, 128), jnp.int32),
            pltpu.VMEM((32, share, piece, width), jnp.float32),
            pltpu.VMEM((33, share, piece, width), jnp.float32),
            pltpu.SemaphoreType.DMA(()),
        ],
    )(table, near(parts.reshape(32, 8, piece, width)))
    back = route(sums, plane_axes)

    def arranged(members):
        found = []
        for e in range(share):
            chosen = members[0]
            for b in range(1, share):
                chosen = jnp.where((mine ^ b) == e, members[b], chosen)
            found.append(chosen)
        return jnp.stack(found)

    query_grad = arranged(query_grads).reshape(share, local_kv, chunk, group, width)
    query_grad = jnp.transpose(query_grad, (2, 0, 1, 3, 4)).reshape(chunk, heads, width)
    local = arranged([m.astype(jnp.float32) for m in own_grads])
    back, query_grad, local = lax.optimization_barrier((back, query_grad, local))
    back = jnp.transpose(back, (1, 0, 2, 3)).reshape(share, -1, width)
    both = (local + back).reshape(kv_heads, 2, chunk, width)
    both = jnp.transpose(both, (1, 2, 0, 3)).astype(low)
    return query_grad, both[0], both[1]


def solution(mesh):
    fine = Mesh(mesh.devices.reshape(2, 8, 2, 4, 2), ("yl", "z", "yh", "x", "c"))
    rows = P(row_axes, None, None)
    return jax.shard_map(
        shards,
        mesh=fine,
        in_specs=(rows, rows, rows, rows, rows, P(), P()),
        out_specs=(rows, rows, rows),
        check_vma=False,
    )
```
